256 devices in a mesh: layer: 8 (over z_hi, y), row: 32 (over x, z_lo, core).
Axes of the slice: x: 4, y: 4, z: 8 (z_hi: 2, z_lo: 4; z = z_hi * 4 + z_lo), core: 2. Of those that a mesh axis runs over, the one named last changes fastest.
Arguments:
- query_grads: bfloat16 [16, 1024, 4096], P('layer', 'row'), may hold values from -6 to 6
- train_grads: bfloat16 [16, 16384, 4096], P('layer', 'row'), may hold values from -0.023925781 to 0.023925781
- left_inverse: float32 [16, 64, 64], P('layer'), may hold values from -0.75 to 0.75
- right_inverse: float32 [16, 64, 64], P('layer'), may hold values from -0.75 to 0.75
Outputs:
- scores: float32 [1024, 16384], P('layer', 'row')
The draws below stay inside these ranges and needn't reach their ends.
All inputs are finite; a program needn't handle non-finite values.
Results may differ from the reference program's by a relative error of at most 0.0029.
Values may be sent and summed in bfloat16 or wider, within the bound.
A program may use at most 128 MiB of HBM per device.

```python
import jax
import jax.numpy as jnp
from jax import lax

PROJ = 64
FEAT = 4096
LAYERS = 16
TRAIN = 16384
QUERIES = 1024


def block_scale(own_key, shape, split, least, largest):
    gain = 1.0
    for position, parts in split:
        draws = jax.random.uniform(jax.random.fold_in(jax.random.fold_in(own_key, 6), position), (parts,), jnp.float32, least / len(split), largest / len(split))
        gain = gain * jnp.repeat(jnp.exp(draws), shape[position] // parts).reshape((-1,) + (1,) * (len(shape) - 1 - position))
    return gain


def bell_draw(own_key, dims, scale, limit, pieces=(), held_as=jnp.bfloat16):
    values = jax.random.normal(own_key, dims, jnp.float32) * scale
    if len(pieces) > 0:
        values = block_scale(own_key, dims, pieces, -0.22, 0.18) * values
    return jnp.clip(values, min=-limit, max=limit).astype(held_as)


def setup_inputs(seed: int = 0) -> dict:
    key_of = jax.random.split(jax.random.key(seed), 5)
    return {
        "query_grads": bell_draw(key_of[0], (LAYERS, QUERIES, FEAT), 1.0, 6.0, ((0, 8), (1, 32))),
        "train_grads": bell_draw(key_of[1], (LAYERS, TRAIN, FEAT), 0.004, 0.023925781, ((0, 8), (1, 32))),
        "left_inverse": bell_draw(key_of[2], (LAYERS, PROJ, PROJ), PROJ ** -0.5, 0.75, ((0, 8),), jnp.float32),
        "right_inverse": bell_draw(key_of[3], (LAYERS, PROJ, PROJ), PROJ ** -0.5, 0.75, ((0, 8),), jnp.float32),
    }


def reference(query_grads, train_grads, left_inverse, right_inverse):
    layers, queries, feat = query_grads.shape
    proj = left_inverse.shape[1]

    def one_layer(total, index):
        query = lax.dynamic_index_in_dim(query_grads, index, 0, keepdims=False)
        train = lax.dynamic_index_in_dim(train_grads, index, 0, keepdims=False)
        left = lax.dynamic_index_in_dim(left_inverse, index, 0, keepdims=False).astype(jnp.float32)
        right = lax.dynamic_index_in_dim(right_inverse, index, 0, keepdims=False).astype(jnp.float32)
        square = query.astype(jnp.float32).reshape(queries, proj, proj)
        rotated = jnp.einsum("ab,qbc,cd->qad", left, square, right, precision=lax.Precision.HIGHEST)
        rotated = rotated.reshape(queries, feat).astype(jnp.bfloat16)
        term = jnp.dot(rotated, train.T, preferred_element_type=jnp.float32)
        return total + term, None

    start = jnp.zeros((queries, train_grads.shape[1]), jnp.float32)
    total, unused = lax.scan(one_layer, start, jnp.arange(layers, dtype=jnp.int32))
    return total
```

```python
import jax
import jax.numpy as jnp
from jax import lax
from jax.experimental import pallas as pl
from jax.experimental.pallas import tpu as pltpu
from jax.sharding import PartitionSpec as P

MESH = pl.DeviceIdType.MESH
NX, NZ, NG, PIECES = 4, 4, 8, 4
STEPS = NZ * PIECES


def kernel(pre_ref, train_ref, out_ref, held, train, acc, own, stage, landed,
           pre_sem, train_sem, zs, zr, zs2, xs, xr, hs, hr, ps, pr, ss, sr):
    g = lax.axis_index("layer")
    row = lax.axis_index("row")
    core = lax.rem(row, 2)
    z = lax.rem(row // 2, NZ)
    x = row // (2 * NZ)
    upper = z // 2
    end = jnp.where(upper == 1, 3 - z, z) == 0
    zl = jnp.where(upper == 1, 3 - z, z)

    def device(xx, zz, cc):
        return (g, (xx * NZ + zz) * 2 + cc)

    right, left = lax.rem(x + 1, NX), lax.rem(x + NX - 1, NX)
    side = z + 1 - 2 * lax.rem(z, 2)
    across = 3 - z

    def held_z(k):
        c = jnp.where(k == 0, zl, jnp.where(k == 1, 1 - zl, k))
        return jnp.where(upper == 1, 3 - c, c)

    half = pre_ref.shape[2] // 2
    rows = pre_ref.shape[1]
    low, high = pl.ds(0, rows // 2), pl.ds(rows // 2, rows // 2)

    def pre_copy(p):
        return pltpu.make_async_copy(
            pre_ref.at[p // 2, :, pl.ds((p % 2) * half, half)],
            held.at[z, p, core, x], pre_sem.at[p])

    def train_copy(p):
        return pltpu.make_async_copy(
            train_ref.at[p // 2, :, pl.ds((p % 2) * half, half)],
            train.at[p], train_sem.at[p])

    for p in range(PIECES):
        pre_copy(p).start()
    for p in range(PIECES):
        train_copy(p).start()

    barrier = pltpu.get_barrier_semaphore()

    def greet(target):
        pl.semaphore_signal(barrier, inc=1, device_id=target, device_id_type=MESH)

    greet(device(right, z, core))
    greet(device(left, z, core))
    greet(device(x, z, 1 - core))
    greet(device(x, side, core))
    for j in range(1, NG):
        greet((lax.rem(g + j, NG), row))

    greet(device(x, across, core))
    pl.semaphore_wait(barrier, 5 + NG - 1)

    def remote(ref, send_sem, recv_sem, target):
        return pltpu.make_async_remote_copy(
            src_ref=ref, dst_ref=ref, send_sem=send_sem, recv_sem=recv_sem,
            device_id=target, device_id_type=MESH)

    def to_side(k, k_there, p):
        return remote(held.at[held_z(k), p, core, x], zs.at[k_there, p], zr.at[k_there, p], device(x, side, core))

    def to_across(k, k_there, p):
        return remote(held.at[held_z(k), p, core, x], zs2.at[k_there, p], zr.at[k_there, p], device(x, across, core))

    def to_x(k, p, d):
        return remote(held.at[held_z(k), p, core, x], xs.at[d, k, p], xr.at[d, k, p],
                      device(right if d == 0 else left, z, core))

    def from_x(k, p, d):
        return remote(held.at[held_z(k), p, core, left if d == 0 else right], xs.at[d, k, p], xr.at[d, k, p],
                      device(right if d == 0 else left, z, core))

    def relay(k, p, d):
        return remote(held.at[held_z(k), p, core, left if d == 0 else right, low if d == 0 else high],
                      hs.at[d, k, p], hr.at[d, k, p], device(right if d == 0 else left, z, core))

    def to_partner(k, p):
        return remote(held.at[held_z(k), p, core], ps.at[k, p], pr.at[k, p], device(x, z, 1 - core))

    def to_owner(k, xx):
        zz = held_z(k)
        owner = 2 * xx + zz // 2
        return pltpu.make_async_remote_copy(
            src_ref=stage.at[k, xx], dst_ref=landed.at[g, lax.rem(zz, 2)],
            send_sem=ss.at[k, xx], recv_sem=sr.at[g, lax.rem(zz, 2)],
            device_id=(owner, row), device_id_type=MESH)

    inner = jnp.logical_not(end)

    for p in range(PIECES):
        pre_copy(p).wait()
        to_side(0, 1, p).start()

        @pl.when(inner)
        def _():
            to_across(0, 2, p).start()

    def part_z(i):
        early = i - 2
        late = i - 4

        @pl.when(jnp.logical_and(inner, jnp.logical_and(early >= 0, early < PIECES)))
        def _():
            to_side(1, 1, early).wait_recv()
            to_across(1, 3, early).start()
            to_across(2, 2, early).wait_recv()
            to_side(2, 2, early).start()

        @pl.when(jnp.logical_and(inner, jnp.logical_and(late >= 0, late < PIECES)))
        def _():
            to_across(3, 3, late).wait_recv()
            to_side(3, 3, late).start()

    def step(i, carry):
        part_z(i)

        @pl.when(i < STEPS)
        def _():
            k, p = i // PIECES, lax.rem(i, PIECES)

            @pl.when(jnp.logical_and(end, k > 0))
            def _():
                to_side(k, k, p).wait_recv()

            to_x(k, p, 0).start()
            to_x(k, p, 1).start()

        @pl.when(jnp.logical_and(i >= 1, i < STEPS + 1))
        def _():
            s = i - 1
            k, p = s // PIECES, lax.rem(s, PIECES)
            from_x(k, p, 0).wait_recv()
            relay(k, p, 0).start()
            from_x(k, p, 1).wait_recv()
            relay(k, p, 1).start()

        @pl.when(jnp.logical_and(i >= 2, i < STEPS + 2))
        def _():
            s = i - 2
            k, p = s // PIECES, lax.rem(s, PIECES)
            relay(k, p, 0).wait_recv()
            relay(k, p, 1).wait_recv()
            to_partner(k, p).start()

        @pl.when(i >= 3)
        def _():
            s = i - 3
            k, p = s // PIECES, lax.rem(s, PIECES)

            @pl.when(k == 0)
            def _():
                train_copy_dyn(p).wait()

            to_partner(k, p).wait_recv()
            block = held[held_z(k), p].reshape(2 * NX * rows, half)
            term = lax.dot_general(block, train[p], (((1,), (1,)), ((), ())),
                                   preferred_element_type=jnp.float32)

            @pl.when(p == 0)
            def _():
                acc[...] = term

            @pl.when(p > 0)
            def _():
                acc[...] += term

            @pl.when(p == PIECES - 1)
            def _():
                zz = held_z(k)
                for xx in range(NX):
                    mine = (2 * xx + zz // 2) == g

                    @pl.when(mine)
                    def _():
                        for c in range(2):
                            own[lax.rem(zz, 2), pl.ds(c * rows, rows), :] = acc[pl.ds((c * NX + xx) * rows, rows), :]

                    @pl.when(jnp.logical_not(mine))
                    def _():
                        for c in range(2):
                            stage[k, xx, pl.ds(c * rows, rows), :] = acc[
                                pl.ds((c * NX + xx) * rows, rows), :].astype(jnp.bfloat16)
                        to_owner(k, xx).start()

        return carry

    def train_copy_dyn(p):
        return pltpu.make_async_copy(train.at[p], train.at[p], train_sem.at[p])

    lax.fori_loop(0, STEPS + 3, step, 0)

    out_ref[...] = own[...].reshape(out_ref.shape)
    for j in range(1, NG):
        src = lax.rem(g + j, NG)
        for b in range(2):
            pltpu.make_async_remote_copy(
                src_ref=stage.at[0, 0], dst_ref=landed.at[src, b], send_sem=ss.at[0, 0], recv_sem=sr.at[src, b],
                device_id=(src, row), device_id_type=MESH).wait_recv()
        out_ref[...] += landed[src].astype(jnp.float32).reshape(out_ref.shape)

    def drain(s, carry):
        k, p = s // PIECES, lax.rem(s, PIECES)
        for d in range(2):
            to_x(k, p, d).wait_send()
            relay(k, p, d).wait_send()
        to_partner(k, p).wait_send()

        @pl.when(k == 0)
        def _():
            to_side(0, 1, p).wait_send()

        @pl.when(inner)
        def _():
            @pl.when(k == 0)
            def _():
                to_across(0, 2, p).wait_send()

            @pl.when(k == 1)
            def _():
                to_across(1, 3, p).wait_send()

            @pl.when(k >= 2)
            def _():
                to_side(k, k, p).wait_send()

        return carry

    lax.fori_loop(0, STEPS, drain, 0)
    for k in range(NZ):
        for xx in range(NX):
            @pl.when((2 * xx + held_z(k) // 2) != g)
            def _():
                to_owner(k, xx).wait_send()


def scores_of(pre, train_grads):
    layers, rows, feat = pre.shape
    train_rows = train_grads.shape[1]
    half = feat // 2
    queries = NX * NZ * 2 * rows
    block = queries // NG
    dma = pltpu.SemaphoreType.DMA
    return pl.pallas_call(
        kernel,
        out_shape=jax.ShapeDtypeStruct((block, train_rows), jnp.float32),
        in_specs=[pl.BlockSpec(memory_space=pl.ANY)] * 2,
        out_specs=pl.BlockSpec(memory_space=pltpu.VMEM),
        scratch_shapes=[
            pltpu.VMEM((NZ, PIECES, 2, NX, rows, half), jnp.bfloat16),
            pltpu.VMEM((PIECES, train_rows, half), jnp.bfloat16),
            pltpu.VMEM((2 * NX * rows, train_rows), jnp.float32),
            pltpu.VMEM((2, 2 * rows, train_rows), jnp.float32),
            pltpu.VMEM((NZ, NX, 2 * rows, train_rows), jnp.bfloat16),
            pltpu.VMEM((NG, 2, 2 * rows, train_rows), jnp.bfloat16),
            dma((PIECES,)), dma((PIECES,)),
            dma((NZ, PIECES)), dma((NZ, PIECES)), dma((NZ, PIECES)),
            dma((2, NZ, PIECES)), dma((2, NZ, PIECES)),
            dma((2, NZ, PIECES)), dma((2, NZ, PIECES)),
            dma((NZ, PIECES)), dma((NZ, PIECES)),
            dma((NZ, NX)), dma((NG, 2)),
        ],
        compiler_params=pltpu.CompilerParams(
            collective_id=0, has_side_effects=True, vmem_limit_bytes=60 * 1024 * 1024),
    )(pre, train_grads)


def on_device(query_grads, train_grads, left_inverse, right_inverse):
    layers, rows, feat = query_grads.shape
    proj = left_inverse.shape[1]
    square = query_grads.astype(jnp.float32).reshape(layers, rows, proj, proj)
    rotated = jnp.einsum(
        "lab,lqbc,lcd->lqad", left_inverse, square, right_inverse, precision=lax.Precision.HIGHEST
    )
    rotated = rotated.reshape(layers, rows, feat).astype(jnp.bfloat16)
    return scores_of(rotated, train_grads)


def solution(mesh):
    placed = (
        P("layer", "row", None),
        P("layer", "row", None),
        P("layer", None, None),
        P("layer", None, None),
    )
    return jax.shard_map(
        on_device, mesh=mesh, in_specs=placed, out_specs=P("layer", "row"), check_vma=False
    )
```

```python
import jax
import jax.numpy as jnp
from jax import lax
from jax.experimental import pallas as pl
from jax.experimental.pallas import tpu as pltpu
from jax.sharding import PartitionSpec as P

MESH = pl.DeviceIdType.MESH
NX, NY, NZ, NG = 4, 4, 4, 8
PIECES = 4
STEPS = NZ * PIECES
XPIECES = 2
XCOLS = 768


def kernel(pre_ref, train_ref, out_ref, held, heldx, train, trainx, acc, mine, stage_y, landed_y, stage_z, landed_z,
           stage_d, landed_d, pre_sem, prex_sem, train_sem, trainx_sem, zs, zs2, zr, xs, xr, hs, hr, ps, pr,
           bs, bs2, br, axs, axr, ahs, ahr, aps, apr, ys, yr, ws, wr, ds, dr):
    g = lax.axis_index("layer")
    row = lax.axis_index("row")
    core = lax.rem(row, 2)
    z = lax.rem(row // 2, NZ)
    x = row // (2 * NZ)
    y = lax.rem(g, NY)
    zh = g // NY
    upper = z // 2
    zl = jnp.where(upper == 1, 3 - z, z)
    end = zl == 0
    inner = jnp.logical_not(end)
    right, left = lax.rem(x + 1, NX), lax.rem(x + NX - 1, NX)
    side = z + 1 - 2 * lax.rem(z, 2)
    across = 3 - z
    rows = pre_ref.shape[1]
    feat = pre_ref.shape[2]
    cols = held.shape[-1]
    low, high = pl.ds(0, rows // 2), pl.ds(rows // 2, rows // 2)

    def device(xx, zz, cc):
        return (g, (xx * NZ + zz) * 2 + cc)

    def held_z(k):
        c = jnp.where(k == 0, zl, jnp.where(k == 1, 1 - zl, k))
        return jnp.where(upper == 1, 3 - c, c)

    def pre_copy(p):
        return pltpu.make_async_copy(
            pre_ref.at[p // 2, :, pl.ds((p % 2) * cols, cols)], held.at[z, p, core, x], pre_sem.at[p])

    def prex_copy(q):
        return pltpu.make_async_copy(
            pre_ref.at[q, :, pl.ds(feat - XCOLS, XCOLS)], heldx.at[z, q, core, x], prex_sem.at[q])

    def train_copy(p):
        return pltpu.make_async_copy(
            train_ref.at[p // 2, :, pl.ds((p % 2) * cols, cols)], train.at[p], train_sem.at[p])

    def trainx_copy(q):
        return pltpu.make_async_copy(
            train_ref.at[q, :, pl.ds(feat - XCOLS, XCOLS)], trainx.at[q], trainx_sem.at[q])

    for q in range(XPIECES):
        prex_copy(q).start()
    for p in range(PIECES):
        pre_copy(p).start()
    for p in range(PIECES):
        train_copy(p).start()
    for q in range(XPIECES):
        trainx_copy(q).start()

    barrier = pltpu.get_barrier_semaphore()

    def greet(target):
        pl.semaphore_signal(barrier, inc=1, device_id=target, device_id_type=MESH)

    greet(device(right, z, core))
    greet(device(left, z, core))
    greet(device(x, z, 1 - core))
    greet(device(x, side, core))
    greet(device(x, across, core))
    for j in range(1, NG):
        greet((lax.rem(g + j, NG), row))
    pl.semaphore_wait(barrier, 5 + NG - 1)

    def remote(ref, send_sem, recv_sem, target):
        return pltpu.make_async_remote_copy(
            src_ref=ref, dst_ref=ref, send_sem=send_sem, recv_sem=recv_sem,
            device_id=target, device_id_type=MESH)

    def xdev(d):
        return device(right if d == 0 else left, z, core)

    def xsrc(d):
        return left if d == 0 else right

    def part(d):
        return low if d == 0 else high

    partner = device(x, z, 1 - core)

    def to_side(k, k_there, p):
        return remote(held.at[held_z(k), p, core, x], zs.at[k_there, p], zr.at[k_there, p], device(x, side, core))

    def to_across(k, k_there, p):
        return remote(held.at[held_z(k), p, core, x], zs2.at[k_there, p], zr.at[k_there, p], device(x, across, core))

    def to_x(k, p, d):
        return remote(held.at[held_z(k), p, core, x], xs.at[d, k, p], xr.at[d, k, p], xdev(d))

    def from_x(k, p, d):
        return remote(held.at[held_z(k), p, core, xsrc(d)], xs.at[d, k, p], xr.at[d, k, p], xdev(d))

    def relay(k, p, d):
        return remote(held.at[held_z(k), p, core, xsrc(d), part(d)], hs.at[d, k, p], hr.at[d, k, p], xdev(d))

    def to_partner(k, p):
        return remote(held.at[held_z(k), p, core], ps.at[k, p], pr.at[k, p], partner)

    def wide_to_x(q, d):
        return remote(heldx.at[z, q, core, x], axs.at[d, q], axr.at[d, q], xdev(d))

    def wide_from_x(q, d):
        return remote(heldx.at[z, q, core, xsrc(d)], axs.at[d, q], axr.at[d, q], xdev(d))

    def wide_relay(q, d):
        return remote(heldx.at[z, q, core, xsrc(d), part(d)], ahs.at[d, q], ahr.at[d, q], xdev(d))

    def wide_to_side(k, k_there, q):
        return remote(heldx.at[held_z(k), q, core], bs.at[k_there, q], br.at[k_there, q], device(x, side, core))

    def wide_to_across(k, k_there, q):
        return remote(heldx.at[held_z(k), q, core], bs2.at[k_there, q], br.at[k_there, q], device(x, across, core))

    def wide_to_partner(k, q):
        return remote(heldx.at[held_z(k), q, core], aps.at[k, q], apr.at[k, q], partner)

    def to_y(k, t, b, dy):
        return pltpu.make_async_remote_copy(
            src_ref=stage_y.at[k, t], dst_ref=landed_y.at[b, y], send_sem=ys.at[k, t], recv_sem=yr.at[b, y],
            device_id=(zh * NY + dy, row), device_id_type=MESH)

    def from_y(b, sy):
        return pltpu.make_async_remote_copy(
            src_ref=stage_y.at[0, 0], dst_ref=landed_y.at[b, sy], send_sem=ys.at[0, 0], recv_sem=yr.at[b, sy],
            device_id=(zh * NY + sy, row), device_id_type=MESH)

    def to_z(b):
        return pltpu.make_async_remote_copy(
            src_ref=stage_z.at[b], dst_ref=landed_z.at[b], send_sem=ws.at[b], recv_sem=wr.at[b],
            device_id=((1 - zh) * NY + y, row), device_id_type=MESH)

    def to_owner(xx, owner):
        return pltpu.make_async_remote_copy(
            src_ref=stage_d.at[xx], dst_ref=landed_d.at[g], send_sem=ds.at[xx], recv_sem=dr.at[g],
            device_id=(owner, row), device_id_type=MESH)

    def from_member(src):
        return pltpu.make_async_remote_copy(
            src_ref=stage_d.at[0], dst_ref=landed_d.at[src], send_sem=ds.at[0], recv_sem=dr.at[src],
            device_id=(src, row), device_id_type=MESH)

    for q in range(XPIECES):
        prex_copy(q).wait()
        for d in range(2):
            wide_to_x(q, d).start()
    for p in range(PIECES):
        pre_copy(p).wait()
        to_side(0, 1, p).start()

        @pl.when(inner)
        def _():
            to_across(0, 2, p).start()

    def along_z(i):
        early = i - 2
        late = i - 4

        @pl.when(jnp.logical_and(inner, jnp.logical_and(early >= 0, early < PIECES)))
        def _():
            to_side(1, 1, early).wait_recv()
            to_across(1, 3, early).start()
            to_across(2, 2, early).wait_recv()
            to_side(2, 2, early).start()

        @pl.when(jnp.logical_and(inner, jnp.logical_and(late >= 0, late < PIECES)))
        def _():
            to_across(3, 3, late).wait_recv()
            to_side(3, 3, late).start()

    def wide(i):
        @pl.when(i == 1)
        def _():
            for q in range(XPIECES):
                for d in range(2):
                    wide_from_x(q, d).wait_recv()
                    wide_relay(q, d).start()

        @pl.when(i == 2)
        def _():
            for q in range(XPIECES):
                for d in range(2):
                    wide_relay(q, d).wait_recv()
                wide_to_side(0, 1, q).start()

                @pl.when(inner)
                def _():
                    wide_to_across(0, 2, q).start()

                wide_to_partner(0, q).start()

        @pl.when(i == 6)
        def _():
            for q in range(XPIECES):
                wide_to_side(1, 1, q).wait_recv()

                @pl.when(inner)
                def _():
                    wide_to_across(1, 3, q).start()
                    wide_to_across(2, 2, q).wait_recv()
                    wide_to_side(2, 2, q).start()
                    wide_to_partner(2, q).start()

                wide_to_partner(1, q).start()

        @pl.when(jnp.logical_and(i == 10, inner))
        def _():
            for q in range(XPIECES):
                wide_to_across(3, 3, q).wait_recv()
                wide_to_side(3, 3, q).start()
                wide_to_partner(3, q).start()

        @pl.when(jnp.logical_and(i == 12, end))
        def _():
            for q in range(XPIECES):
                wide_to_side(2, 2, q).wait_recv()
                wide_to_partner(2, q).start()

        @pl.when(jnp.logical_and(i == 16, end))
        def _():
            for q in range(XPIECES):
                wide_to_side(3, 3, q).wait_recv()
                wide_to_partner(3, q).start()

    def sums_of(xx):
        return [acc[pl.ds((c * NX + xx) * rows, rows), :] for c in range(2)]

    def send_sums(k):
        zz = held_z(k)
        b = lax.rem(zz, 2)

        @pl.when(k < NZ - 1)
        def _():
            for t in range(2):
                dy = 2 * t + zz // 2

                @pl.when(dy == y)
                def _():
                    for h in range(2):
                        for c, value in enumerate(sums_of(2 * h + t)):
                            mine[b, h, pl.ds(c * rows, rows), :] = value

                @pl.when(dy != y)
                def _():
                    for h in range(2):
                        for c, value in enumerate(sums_of(2 * h + t)):
                            stage_y[k, t, h, pl.ds(c * rows, rows), :] = value.astype(jnp.bfloat16)
                    to_y(k, t, b, dy).start()

        @pl.when(k == NZ - 1)
        def _():
            for xx in range(NX):
                owner = 2 * xx + zz // 2

                @pl.when(owner == g)
                def _():
                    for c, value in enumerate(sums_of(xx)):
                        mine[b, zh, pl.ds(c * rows, rows), :] = value

                @pl.when(owner != g)
                def _():
                    for c, value in enumerate(sums_of(xx)):
                        stage_d[xx, pl.ds(c * rows, rows), :] = value.astype(jnp.bfloat16)
                    to_owner(xx, owner).start()

    def reduce_y(i):
        k = (i - 9) // PIECES

        @pl.when(jnp.logical_and(i >= 9, jnp.logical_and(lax.rem(i - 9 + PIECES, PIECES) == 0, k < NZ - 1)))
        def _():
            zz = held_z(k)
            b = lax.rem(zz, 2)

            @pl.when(zz // 2 == lax.rem(y, 2))
            def _():
                for j in range(1, NY):
                    from_y(b, lax.rem(y + j, NY)).wait_recv()

                def total(h):
                    value = mine[b, h]
                    for j in range(1, NY):
                        value = value + landed_y[b, lax.rem(y + j, NY), h].astype(jnp.float32)
                    return value

                stage_z[b] = total(1 - zh).astype(jnp.bfloat16)
                to_z(b).start()
                mine[b, zh] = total(zh)

    def step(i, carry):
        along_z(i)
        wide(i)

        @pl.when(i < STEPS)
        def _():
            k, p = i // PIECES, lax.rem(i, PIECES)

            @pl.when(jnp.logical_and(end, k > 0))
            def _():
                to_side(k, k, p).wait_recv()

            to_x(k, p, 0).start()
            to_x(k, p, 1).start()

        @pl.when(jnp.logical_and(i >= 1, i < STEPS + 1))
        def _():
            s = i - 1
            k, p = s // PIECES, lax.rem(s, PIECES)
            from_x(k, p, 0).wait_recv()
            relay(k, p, 0).start()
            from_x(k, p, 1).wait_recv()
            relay(k, p, 1).start()

        @pl.when(jnp.logical_and(i >= 2, i < STEPS + 2))
        def _():
            s = i - 2
            k, p = s // PIECES, lax.rem(s, PIECES)
            relay(k, p, 0).wait_recv()
            relay(k, p, 1).wait_recv()
            to_partner(k, p).start()

        @pl.when(i >= 3)
        def _():
            s = i - 3
            k, p = s // PIECES, lax.rem(s, PIECES)

            def product(lhs, rhs):
                return lax.dot_general(lhs.reshape(2 * NX * rows, lhs.shape[-1]), rhs, (((1,), (1,)), ((), ())),
                                       preferred_element_type=jnp.float32)

            @pl.when(p == 0)
            def _():
                for q in range(XPIECES):
                    @pl.when(k == 0)
                    def _():
                        trainx_copy(q).wait()

            @pl.when(k == 0)
            def _():
                pltpu.make_async_copy(train.at[p], train.at[p], train_sem.at[p]).wait()

            to_partner(k, p).wait_recv()
            term = product(held[held_z(k), p], train[p])

            @pl.when(p == 0)
            def _():
                acc[...] = term

            @pl.when(p > 0)
            def _():
                acc[...] += term

            @pl.when(p == PIECES - 1)
            def _():
                for q in range(XPIECES):
                    wide_to_partner(k, q).wait_recv()
                    acc[...] += product(heldx[held_z(k), q], trainx[q])
                send_sums(k)

        reduce_y(i)
        return carry

    lax.fori_loop(0, STEPS + 3, step, 0)

    late_owner = lax.rem(y, 2) != upper
    last_b = lax.rem(held_z(NZ - 1), 2)
    block = 2 * rows
    for b in range(2):
        direct = jnp.logical_and(late_owner, last_b == b)
        place = pl.ds(b * block, block)

        @pl.when(jnp.logical_not(direct))
        def _():
            to_z(b).wait_recv()
            out_ref[place, :] = mine[b, zh] + landed_z[b].astype(jnp.float32)

        @pl.when(direct)
        def _():
            out_ref[place, :] = mine[b, zh]
            for j in range(1, NG):
                src = lax.rem(g + j, NG)
                from_member(src).wait_recv()
                out_ref[place, :] += landed_d[src].astype(jnp.float32)

    def drain(s, carry):
        k, p = s // PIECES, lax.rem(s, PIECES)
        for d in range(2):
            to_x(k, p, d).wait_send()
            relay(k, p, d).wait_send()
        to_partner(k, p).wait_send()

        @pl.when(k == 0)
        def _():
            to_side(0, 1, p).wait_send()

        @pl.when(inner)
        def _():
            @pl.when(k == 0)
            def _():
                to_across(0, 2, p).wait_send()

            @pl.when(k == 1)
            def _():
                to_across(1, 3, p).wait_send()

            @pl.when(k >= 2)
            def _():
                to_side(k, k, p).wait_send()

        return carry

    lax.fori_loop(0, STEPS, drain, 0)
    for q in range(XPIECES):
        for d in range(2):
            wide_to_x(q, d).wait_send()
            wide_relay(q, d).wait_send()
        wide_to_side(0, 1, q).wait_send()
        for k in range(NZ):
            wide_to_partner(k, q).wait_send()

        @pl.when(inner)
        def _():
            wide_to_across(0, 2, q).wait_send()
            wide_to_across(1, 3, q).wait_send()
            wide_to_side(2, 2, q).wait_send()
            wide_to_side(3, 3, q).wait_send()

    for k in range(NZ - 1):
        zz = held_z(k)
        for t in range(2):
            @pl.when(2 * t + zz // 2 != y)
            def _():
                to_y(k, t, 0, 0).wait_send()

    for b in range(2):
        @pl.when(jnp.logical_not(jnp.logical_and(late_owner, last_b == b)))
        def _():
            to_z(b).wait_send()

    for xx in range(NX):
        @pl.when(2 * xx + held_z(NZ - 1) // 2 != g)
        def _():
            to_owner(xx, 0).wait_send()


def scores_of(pre, train_grads):
    layers, rows, feat = pre.shape
    train_rows = train_grads.shape[1]
    cols = (feat - XCOLS) * layers // PIECES
    block = NX * NZ * 2 * rows // NG
    dma = pltpu.SemaphoreType.DMA
    bf16, f32 = jnp.bfloat16, jnp.float32
    return pl.pallas_call(
        kernel,
        out_shape=jax.ShapeDtypeStruct((block, train_rows), f32),
        in_specs=[pl.BlockSpec(memory_space=pl.ANY)] * 2,
        out_specs=pl.BlockSpec(memory_space=pltpu.VMEM),
        scratch_shapes=[
            pltpu.VMEM((NZ, PIECES, 2, NX, rows, cols), bf16),
            pltpu.VMEM((NZ, XPIECES, 2, NX, rows, XCOLS), bf16),
            pltpu.VMEM((PIECES, train_rows, cols), bf16),
            pltpu.VMEM((XPIECES, train_rows, XCOLS), bf16),
            pltpu.VMEM((2 * NX * rows, train_rows), f32),
            pltpu.VMEM((2, 2, 2 * rows, train_rows), f32),
            pltpu.VMEM((NZ - 1, 2, 2, 2 * rows, train_rows), bf16),
            pltpu.VMEM((2, NY, 2, 2 * rows, train_rows), bf16),
            pltpu.VMEM((2, 2 * rows, train_rows), bf16),
            pltpu.VMEM((2, 2 * rows, train_rows), bf16),
            pltpu.VMEM((NX, 2 * rows, train_rows), bf16),
            pltpu.VMEM((NG, 2 * rows, train_rows), bf16),
            dma((PIECES,)), dma((XPIECES,)), dma((PIECES,)), dma((XPIECES,)),
            dma((NZ, PIECES)), dma((NZ, PIECES)), dma((NZ, PIECES)),
            dma((2, NZ, PIECES)), dma((2, NZ, PIECES)), dma((2, NZ, PIECES)), dma((2, NZ, PIECES)),
            dma((NZ, PIECES)), dma((NZ, PIECES)),
            dma((NZ, XPIECES)), dma((NZ, XPIECES)), dma((NZ, XPIECES)),
            dma((2, XPIECES)), dma((2, XPIECES)), dma((2, XPIECES)), dma((2, XPIECES)),
            dma((NZ, XPIECES)), dma((NZ, XPIECES)),
            dma((NZ - 1, 2)), dma((2, NY)), dma((2,)), dma((2,)), dma((NX,)), dma((NG,)),
        ],
        compiler_params=pltpu.CompilerParams(
            collective_id=0, has_side_effects=True, vmem_limit_bytes=60 * 1024 * 1024),
    )(pre, train_grads)


def on_device(query_grads, train_grads, left_inverse, right_inverse):
    layers, rows, feat = query_grads.shape
    proj = left_inverse.shape[1]
    square = query_grads.astype(jnp.float32).reshape(layers, rows, proj, proj)
    rotated = jnp.einsum(
        "lab,lqbc,lcd->lqad", left_inverse, square, right_inverse, precision=lax.Precision.HIGHEST
    )
    rotated = rotated.reshape(layers, rows, feat).astype(jnp.bfloat16)
    return scores_of(rotated, train_grads)


def solution(mesh):
    placed = (
        P("layer", "row", None),
        P("layer", "row", None),
        P("layer", None, None),
        P("layer", None, None),
    )
    return jax.shard_map(
        on_device, mesh=mesh, in_specs=placed, out_specs=P("layer", "row"), check_vma=False
    )
```

```python
import jax
import jax.numpy as jnp
from jax import lax
from jax.experimental import pallas as pl
from jax.experimental.pallas import tpu as pltpu
from jax.sharding import PartitionSpec as P

MESH = pl.DeviceIdType.MESH
NX, NY, NZ, NG = 4, 4, 4, 8
PIECES = 4
STEPS = NZ * PIECES
XPIECES = 2
XCOLS = 768
AT_B, AT_C, AT_D, AT_SUM = 2, 4, 5, 11


def split(value):
    high = value.astype(jnp.bfloat16)
    return high, (value - high.astype(jnp.float32)).astype(jnp.bfloat16)


def matmul(a, b):
    return jnp.dot(a, b, preferred_element_type=jnp.float32)


def precondition(query, left, right, turned, result, store):
    rows, feat = query.shape
    proj = left.shape[0]
    pairs = proj // 2
    lanes = 2 * proj
    bf16, f32 = jnp.bfloat16, jnp.float32

    def iota(shape, axis):
        return lax.broadcasted_iota(jnp.int32, shape, axis)

    def ones_where(mask):
        return jnp.where(mask, 1.0, 0.0).astype(bf16)

    twice = ones_where(iota((proj, lanes), 1) % proj == iota((proj, lanes), 0))
    same_half = iota((lanes, lanes), 0) // proj == iota((lanes, lanes), 1) // proj

    def block_diagonal(part):
        wide = matmul(part, twice)
        return jnp.where(same_half, jnp.concatenate([wide, wide], axis=0), 0.0).astype(bf16)

    right_high, right_low = split(right[...])
    factor = jnp.concatenate([block_diagonal(right_high), block_diagonal(right_low)], axis=1)
    stacked = jnp.concatenate([query[:, lanes * j:lanes * (j + 1)] for j in range(pairs)], axis=0)
    both = matmul(stacked, factor)
    turned[...] = both[:, :lanes] + both[:, lanes:]

    pick = ones_where(iota((proj, proj), 1) == 2 * (iota((proj, proj), 0) % pairs) + iota((proj, proj), 0) // pairs)
    b, place = iota((proj, proj), 0), iota((proj, proj), 1)
    other, j = place // pairs, place % pairs
    even = ones_where(b == 2 * j + other)
    odd = ones_where(b == 2 * j + 1 - other)
    upper_rows = iota((proj, proj), 0) < pairs

    def arranged(part):
        picked = matmul(pick, part).astype(bf16)
        return jnp.where(upper_rows, matmul(picked, even), matmul(picked, odd)).astype(bf16)

    left_high, left_low = split(left[...])
    high, low = arranged(left_high), arranged(left_low)
    weights = jnp.concatenate([
        jnp.concatenate([high, high], axis=1),
        jnp.concatenate([low, jnp.zeros_like(low)], axis=1)], axis=0)
    group = 8
    first_half = iota((pairs, lanes * group), 1) % lanes < proj
    for start in range(0, rows, group):
        own = [turned[pl.ds(q, pairs, stride=rows), :] for q in range(start, start + group)]
        own_high, own_low = split(jnp.concatenate(own, axis=1))
        rolled_high, rolled_low = split(jnp.concatenate([pltpu.roll(v, proj, 1) for v in own], axis=1))
        value = matmul(weights, jnp.concatenate([own_high, rolled_high, own_low, rolled_low], axis=0))
        value = value[:proj] + value[proj:]
        value = jnp.where(first_half, value[:pairs], value[pairs:])
        for q in range(group):
            result[pl.ds((start + q) * pairs, pairs), :] = value[:, lanes * q:lanes * (q + 1)]
    for i in range(pairs):
        store(i, result[pl.ds(i, rows, stride=pairs), :].astype(bf16))


def kernel(query_ref, left_ref, right_ref, train_ref, out_ref, query, left_v, right_v, turned, result, held, heldx, train, trainx, acc, mine, stage_y, landed_y, stage_z, landed_z,
           stage_d, landed_d, in_sem, train_sem, trainx_sem, zs, zs2, zr, xs, xr, hs, hr, ps, pr,
           bs, bs2, br, axs, axr, ahs, ahr, aps, apr, ys, yr, ws, wr, ds, dr):
    g = lax.axis_index("layer")
    row = lax.axis_index("row")
    core = lax.rem(row, 2)
    z = lax.rem(row // 2, NZ)
    x = row // (2 * NZ)
    y = lax.rem(g, NY)
    zh = g // NY
    upper = z // 2
    zl = jnp.where(upper == 1, 3 - z, z)
    end = zl == 0
    inner = jnp.logical_not(end)
    right, left = lax.rem(x + 1, NX), lax.rem(x + NX - 1, NX)
    side = z + 1 - 2 * lax.rem(z, 2)
    across = 3 - z
    layers, rows, feat = query_ref.shape
    cols = held.shape[-1]
    low, high = pl.ds(0, rows // 2), pl.ds(rows // 2, rows // 2)

    def device(xx, zz, cc):
        return (g, (xx * NZ + zz) * 2 + cc)

    def held_z(k):
        c = jnp.where(k == 0, zl, jnp.where(k == 1, 1 - zl, k))
        return jnp.where(upper == 1, 3 - c, c)

    def in_copies():
        return [pltpu.make_async_copy(src, dst, in_sem.at[n]) for n, (src, dst) in enumerate(
            ((query_ref, query), (left_ref, left_v), (right_ref, right_v)))]

    def train_copy(p):
        return pltpu.make_async_copy(
            train_ref.at[p // 2, :, pl.ds((p % 2) * cols, cols)], train.at[p], train_sem.at[p])

    def trainx_copy(q):
        return pltpu.make_async_copy(
            train_ref.at[q, :, pl.ds(feat - XCOLS, XCOLS)], trainx.at[q], trainx_sem.at[q])

    for copy in in_copies():
        copy.start()
    for p in range(PIECES):
        train_copy(p).start()
    for q in range(XPIECES):
        trainx_copy(q).start()

    barrier = pltpu.get_barrier_semaphore()

    def greet(target):
        pl.semaphore_signal(barrier, inc=1, device_id=target, device_id_type=MESH)

    greet(device(right, z, core))
    greet(device(left, z, core))
    greet(device(x, z, 1 - core))
    greet(device(x, side, core))
    greet(device(x, across, core))
    for j in range(1, NG):
        greet((lax.rem(g + j, NG), row))

    for copy in in_copies():
        copy.wait()
    tiles = cols // 128
    for layer in range(layers):
        def store(i, value):
            n, at = i // tiles, (i % tiles) * 128
            if n < PIECES // layers:
                held[z, layer * (PIECES // layers) + n, core, x, :, at:at + 128] = value
            else:
                heldx[z, layer, core, x, :, at:at + 128] = value

        precondition(query.at[layer], left_v.at[layer], right_v.at[layer], turned, result, store)

    pl.semaphore_wait(barrier, 5 + NG - 1)

    def remote(ref, send_sem, recv_sem, target):
        return pltpu.make_async_remote_copy(
            src_ref=ref, dst_ref=ref, send_sem=send_sem, recv_sem=recv_sem,
            device_id=target, device_id_type=MESH)

    def xdev(d):
        return device(right if d == 0 else left, z, core)

    def xsrc(d):
        return left if d == 0 else right

    def part(d):
        return low if d == 0 else high

    partner = device(x, z, 1 - core)

    def to_side(k, k_there, p):
        return remote(held.at[held_z(k), p, core, x], zs.at[k_there, p], zr.at[k_there, p], device(x, side, core))

    def to_across(k, k_there, p):
        return remote(held.at[held_z(k), p, core, x], zs2.at[k_there, p], zr.at[k_there, p], device(x, across, core))

    def to_x(k, p, d):
        return remote(held.at[held_z(k), p, core, x], xs.at[d, k, p], xr.at[d, k, p], xdev(d))

    def from_x(k, p, d):
        return remote(held.at[held_z(k), p, core, xsrc(d)], xs.at[d, k, p], xr.at[d, k, p], xdev(d))

    def relay(k, p, d):
        return remote(held.at[held_z(k), p, core, xsrc(d), part(d)], hs.at[d, k, p], hr.at[d, k, p], xdev(d))

    def to_partner(k, p):
        return remote(held.at[held_z(k), p, core], ps.at[k, p], pr.at[k, p], partner)

    def wide_to_x(q, d):
        return remote(heldx.at[z, q, core, x], axs.at[d, q], axr.at[d, q], xdev(d))

    def wide_from_x(q, d):
        return remote(heldx.at[z, q, core, xsrc(d)], axs.at[d, q], axr.at[d, q], xdev(d))

    def wide_relay(q, d):
        return remote(heldx.at[z, q, core, xsrc(d), part(d)], ahs.at[d, q], ahr.at[d, q], xdev(d))

    def wide_to_side(k, k_there, q):
        return remote(heldx.at[held_z(k), q, core], bs.at[k_there, q], br.at[k_there, q], device(x, side, core))

    def wide_to_across(k, k_there, q):
        return remote(heldx.at[held_z(k), q, core], bs2.at[k_there, q], br.at[k_there, q], device(x, across, core))

    def wide_to_partner(k, q):
        return remote(heldx.at[held_z(k), q, core], aps.at[k, q], apr.at[k, q], partner)

    def to_y(k, t, b, dy):
        return pltpu.make_async_remote_copy(
            src_ref=stage_y.at[k, t], dst_ref=landed_y.at[b, y], send_sem=ys.at[k, t], recv_sem=yr.at[b, y],
            device_id=(zh * NY + dy, row), device_id_type=MESH)

    def from_y(b, sy):
        return pltpu.make_async_remote_copy(
            src_ref=stage_y.at[0, 0], dst_ref=landed_y.at[b, sy], send_sem=ys.at[0, 0], recv_sem=yr.at[b, sy],
            device_id=(zh * NY + sy, row), device_id_type=MESH)

    def to_z(b):
        return pltpu.make_async_remote_copy(
            src_ref=stage_z.at[b], dst_ref=landed_z.at[b], send_sem=ws.at[b], recv_sem=wr.at[b],
            device_id=((1 - zh) * NY + y, row), device_id_type=MESH)

    def to_owner(xx, owner):
        return pltpu.make_async_remote_copy(
            src_ref=stage_d.at[xx], dst_ref=landed_d.at[g], send_sem=ds.at[xx], recv_sem=dr.at[g],
            device_id=(owner, row), device_id_type=MESH)

    def from_member(src):
        return pltpu.make_async_remote_copy(
            src_ref=stage_d.at[0], dst_ref=landed_d.at[src], send_sem=ds.at[0], recv_sem=dr.at[src],
            device_id=(src, row), device_id_type=MESH)

    for q in range(XPIECES):
        for d in range(2):
            wide_to_x(q, d).start()
    for p in range(PIECES):
        to_side(0, 1, p).start()

        @pl.when(inner)
        def _():
            to_across(0, 2, p).start()

    def along_z(i):
        early = i - 4
        late = i - 9

        @pl.when(jnp.logical_and(inner, jnp.logical_and(early >= 0, early < PIECES)))
        def _():
            to_side(1, 1, early).wait_recv()
            to_across(1, 3, early).start()
            to_across(2, 2, early).wait_recv()
            to_side(2, 2, early).start()

        @pl.when(jnp.logical_and(inner, jnp.logical_and(late >= 0, late < PIECES)))
        def _():
            to_across(3, 3, late).wait_recv()
            to_side(3, 3, late).start()

    def wide(i):
        @pl.when(i == 1)
        def _():
            for q in range(XPIECES):
                for d in range(2):
                    wide_from_x(q, d).wait_recv()
                    wide_relay(q, d).start()

        @pl.when(i == 3)
        def _():
            for q in range(XPIECES):
                for d in range(2):
                    wide_relay(q, d).wait_recv()
                wide_to_side(0, 1, q).start()

                @pl.when(inner)
                def _():
                    wide_to_across(0, 2, q).start()

                wide_to_partner(0, q).start()

        @pl.when(i == 8)
        def _():
            for q in range(XPIECES):
                @pl.when(inner)
                def _():
                    wide_to_across(2, 2, q).wait_recv()
                    wide_to_side(2, 2, q).start()
                    wide_to_partner(2, q).start()

        @pl.when(i == 9)
        def _():
            for q in range(XPIECES):
                wide_to_side(1, 1, q).wait_recv()

                @pl.when(inner)
                def _():
                    wide_to_across(1, 3, q).start()

                wide_to_partner(1, q).start()

        @pl.when(jnp.logical_and(i == 14, inner))
        def _():
            for q in range(XPIECES):
                wide_to_across(3, 3, q).wait_recv()
                wide_to_side(3, 3, q).start()
                wide_to_partner(3, q).start()

        @pl.when(jnp.logical_and(i == 15, end))
        def _():
            for q in range(XPIECES):
                wide_to_side(2, 2, q).wait_recv()
                wide_to_partner(2, q).start()

        @pl.when(jnp.logical_and(i == 17, end))
        def _():
            for q in range(XPIECES):
                wide_to_side(3, 3, q).wait_recv()
                wide_to_partner(3, q).start()

    def sums_of(xx):
        return [acc[pl.ds((c * NX + xx) * rows, rows), :] for c in range(2)]

    def send_sums(k):
        zz = held_z(k)
        b = lax.rem(zz, 2)

        @pl.when(k < NZ - 1)
        def _():
            for t in range(2):
                dy = 2 * t + zz // 2

                @pl.when(dy == y)
                def _():
                    for h in range(2):
                        for c, value in enumerate(sums_of(2 * h + t)):
                            mine[b, h, pl.ds(c * rows, rows), :] = value

                @pl.when(dy != y)
                def _():
                    for h in range(2):
                        for c, value in enumerate(sums_of(2 * h + t)):
                            stage_y[k, t, h, pl.ds(c * rows, rows), :] = value.astype(jnp.bfloat16)
                    to_y(k, t, b, dy).start()

        @pl.when(k == NZ - 1)
        def _():
            for xx in range(NX):
                owner = 2 * xx + zz // 2

                @pl.when(owner == g)
                def _():
                    for c, value in enumerate(sums_of(xx)):
                        mine[b, zh, pl.ds(c * rows, rows), :] = value

                @pl.when(owner != g)
                def _():
                    for c, value in enumerate(sums_of(xx)):
                        stage_d[xx, pl.ds(c * rows, rows), :] = value.astype(jnp.bfloat16)
                    to_owner(xx, owner).start()

    def reduce_y(i):
        k = (i - AT_SUM) // PIECES

        @pl.when(jnp.logical_and(i >= AT_SUM, jnp.logical_and(lax.rem(i - AT_SUM + NZ * PIECES, PIECES) == 0, k < NZ - 1)))
        def _():
            zz = held_z(k)
            b = lax.rem(zz, 2)

            @pl.when(zz // 2 == lax.rem(y, 2))
            def _():
                for j in range(1, NY):
                    from_y(b, lax.rem(y + j, NY)).wait_recv()

                def total(h):
                    value = mine[b, h]
                    for j in range(1, NY):
                        value = value + landed_y[b, lax.rem(y + j, NY), h].astype(jnp.float32)
                    return value

                stage_z[b] = total(1 - zh).astype(jnp.bfloat16)
                to_z(b).start()
                mine[b, zh] = total(zh)

    def step(i, carry):
        along_z(i)
        wide(i)

        @pl.when(i < STEPS)
        def _():
            k, p = i // PIECES, lax.rem(i, PIECES)

            @pl.when(jnp.logical_and(end, k > 0))
            def _():
                to_side(k, k, p).wait_recv()

            to_x(k, p, 0).start()
            to_x(k, p, 1).start()

        @pl.when(jnp.logical_and(i >= AT_B, i < STEPS + AT_B))
        def _():
            s = i - AT_B
            k, p = s // PIECES, lax.rem(s, PIECES)
            from_x(k, p, 0).wait_recv()
            relay(k, p, 0).start()
            from_x(k, p, 1).wait_recv()
            relay(k, p, 1).start()

        @pl.when(jnp.logical_and(i >= AT_C, i < STEPS + AT_C))
        def _():
            s = i - AT_C
            k, p = s // PIECES, lax.rem(s, PIECES)
            relay(k, p, 0).wait_recv()
            relay(k, p, 1).wait_recv()
            to_partner(k, p).start()

        @pl.when(i >= AT_D)
        def _():
            s = i - AT_D
            k, p = s // PIECES, lax.rem(s, PIECES)

            def product(lhs, rhs):
                return lax.dot_general(lhs.reshape(2 * NX * rows, lhs.shape[-1]), rhs, (((1,), (1,)), ((), ())),
                                       preferred_element_type=jnp.float32)

            @pl.when(p == 0)
            def _():
                for q in range(XPIECES):
                    @pl.when(k == 0)
                    def _():
                        trainx_copy(q).wait()

            @pl.when(k == 0)
            def _():
                pltpu.make_async_copy(train.at[p], train.at[p], train_sem.at[p]).wait()

            to_partner(k, p).wait_recv()
            term = product(held[held_z(k), p], train[p])

            @pl.when(p == 0)
            def _():
                acc[...] = term

            @pl.when(p > 0)
            def _():
                acc[...] += term

            @pl.when(p == PIECES - 1)
            def _():
                for q in range(XPIECES):
                    wide_to_partner(k, q).wait_recv()
                    acc[...] += product(heldx[held_z(k), q], trainx[q])
                send_sums(k)

        reduce_y(i)
        return carry

    lax.fori_loop(0, STEPS + AT_D, step, 0)

    late_owner = lax.rem(y, 2) != upper
    last_b = lax.rem(held_z(NZ - 1), 2)
    block = 2 * rows
    for b in range(2):
        direct = jnp.logical_and(late_owner, last_b == b)
        place = pl.ds(b * block, block)

        @pl.when(jnp.logical_not(direct))
        def _():
            to_z(b).wait_recv()
            out_ref[place, :] = mine[b, zh] + landed_z[b].astype(jnp.float32)

        @pl.when(direct)
        def _():
            out_ref[place, :] = mine[b, zh]
            for j in range(1, NG):
                src = lax.rem(g + j, NG)
                from_member(src).wait_recv()
                out_ref[place, :] += landed_d[src].astype(jnp.float32)

    def drain(s, carry):
        k, p = s // PIECES, lax.rem(s, PIECES)
        for d in range(2):
            to_x(k, p, d).wait_send()
            relay(k, p, d).wait_send()
        to_partner(k, p).wait_send()

        @pl.when(k == 0)
        def _():
            to_side(0, 1, p).wait_send()

        @pl.when(inner)
        def _():
            @pl.when(k == 0)
            def _():
                to_across(0, 2, p).wait_send()

            @pl.when(k == 1)
            def _():
                to_across(1, 3, p).wait_send()

            @pl.when(k >= 2)
            def _():
                to_side(k, k, p).wait_send()

        return carry

    lax.fori_loop(0, STEPS, drain, 0)
    for q in range(XPIECES):
        for d in range(2):
            wide_to_x(q, d).wait_send()
            wide_relay(q, d).wait_send()
        wide_to_side(0, 1, q).wait_send()
        for k in range(NZ):
            wide_to_partner(k, q).wait_send()

        @pl.when(inner)
        def _():
            wide_to_across(0, 2, q).wait_send()
            wide_to_across(1, 3, q).wait_send()
            wide_to_side(2, 2, q).wait_send()
            wide_to_side(3, 3, q).wait_send()

    for k in range(NZ - 1):
        zz = held_z(k)
        for t in range(2):
            @pl.when(2 * t + zz // 2 != y)
            def _():
                to_y(k, t, 0, 0).wait_send()

    for b in range(2):
        @pl.when(jnp.logical_not(jnp.logical_and(late_owner, last_b == b)))
        def _():
            to_z(b).wait_send()

    for xx in range(NX):
        @pl.when(2 * xx + held_z(NZ - 1) // 2 != g)
        def _():
            to_owner(xx, 0).wait_send()


def on_device(query_grads, train_grads, left_inverse, right_inverse):
    layers, rows, feat = query_grads.shape
    proj = left_inverse.shape[1]
    train_rows = train_grads.shape[1]
    cols = (feat - XCOLS) * layers // PIECES
    block = NX * NZ * 2 * rows // NG
    dma = pltpu.SemaphoreType.DMA
    bf16, f32 = jnp.bfloat16, jnp.float32
    return pl.pallas_call(
        kernel,
        out_shape=jax.ShapeDtypeStruct((block, train_rows), f32),
        in_specs=[pl.BlockSpec(memory_space=pl.ANY)] * 4,
        out_specs=pl.BlockSpec(memory_space=pltpu.VMEM),
        scratch_shapes=[
            pltpu.VMEM((layers, rows, feat), bf16),
            pltpu.VMEM((layers, proj, proj), f32),
            pltpu.VMEM((layers, proj, proj), f32),
            pltpu.VMEM((rows * proj // 2, 2 * proj), f32),
            pltpu.VMEM((rows * proj // 2, 2 * proj), f32),
            pltpu.VMEM((NZ, PIECES, 2, NX, rows, cols), bf16),
            pltpu.VMEM((NZ, XPIECES, 2, NX, rows, XCOLS), bf16),
            pltpu.VMEM((PIECES, train_rows, cols), bf16),
            pltpu.VMEM((XPIECES, train_rows, XCOLS), bf16),
            pltpu.VMEM((2 * NX * rows, train_rows), f32),
            pltpu.VMEM((2, 2, 2 * rows, train_rows), f32),
            pltpu.VMEM((NZ - 1, 2, 2, 2 * rows, train_rows), bf16),
            pltpu.VMEM((2, NY, 2, 2 * rows, train_rows), bf16),
            pltpu.VMEM((2, 2 * rows, train_rows), bf16),
            pltpu.VMEM((2, 2 * rows, train_rows), bf16),
            pltpu.VMEM((NX, 2 * rows, train_rows), bf16),
            pltpu.VMEM((NG, 2 * rows, train_rows), bf16),
            dma((3,)), dma((PIECES,)), dma((XPIECES,)),
            dma((NZ, PIECES)), dma((NZ, PIECES)), dma((NZ, PIECES)),
            dma((2, NZ, PIECES)), dma((2, NZ, PIECES)), dma((2, NZ, PIECES)), dma((2, NZ, PIECES)),
            dma((NZ, PIECES)), dma((NZ, PIECES)),
            dma((NZ, XPIECES)), dma((NZ, XPIECES)), dma((NZ, XPIECES)),
            dma((2, XPIECES)), dma((2, XPIECES)), dma((2, XPIECES)), dma((2, XPIECES)),
            dma((NZ, XPIECES)), dma((NZ, XPIECES)),
            dma((NZ - 1, 2)), dma((2, NY)), dma((2,)), dma((2,)), dma((NX,)), dma((NG,)),
        ],
        compiler_params=pltpu.CompilerParams(
            collective_id=0, has_side_effects=True, vmem_limit_bytes=60 * 1024 * 1024),
    )(query_grads, left_inverse, right_inverse, train_grads)


def solution(mesh):
    placed = (
        P("layer", "row", None),
        P("layer", "row", None),
        P("layer", None, None),
        P("layer", None, None),
    )
    return jax.shard_map(
        on_device, mesh=mesh, in_specs=placed, out_specs=P("layer", "row"), check_vma=False
    )
```

```python
import jax
import jax.numpy as jnp
from jax import lax
from jax.experimental import pallas as pl
from jax.experimental.pallas import tpu as pltpu
from jax.sharding import PartitionSpec as P

MESH = pl.DeviceIdType.MESH
NX, NY, NZ, NG = 4, 4, 4, 8
PIECES = 4
STEPS = NZ * PIECES
XPIECES = 2
XCOLS = 768
HALVES = 2
AT_B, AT_C, AT_D, AT_SUM = 2, 4, 5, 8


def split(value):
    high = value.astype(jnp.bfloat16)
    return high, (value - high.astype(jnp.float32)).astype(jnp.bfloat16)


def matmul(a, b):
    return jnp.dot(a, b, preferred_element_type=jnp.float32)


def precondition(query, left, right, turned, result, store):
    rows, feat = query.shape
    proj = left.shape[0]
    pairs = proj // 2
    lanes = 2 * proj
    bf16, f32 = jnp.bfloat16, jnp.float32

    def iota(shape, axis):
        return lax.broadcasted_iota(jnp.int32, shape, axis)

    def ones_where(mask):
        return jnp.where(mask, 1.0, 0.0).astype(bf16)

    twice = ones_where(iota((proj, lanes), 1) % proj == iota((proj, lanes), 0))
    same_half = iota((lanes, lanes), 0) // proj == iota((lanes, lanes), 1) // proj

    def block_diagonal(part):
        wide = matmul(part, twice)
        return jnp.where(same_half, jnp.concatenate([wide, wide], axis=0), 0.0).astype(bf16)

    right_high, right_low = split(right[...])
    factor = jnp.concatenate([block_diagonal(right_high), block_diagonal(right_low)], axis=1)
    stacked = jnp.concatenate([query[:, lanes * j:lanes * (j + 1)] for j in range(pairs)], axis=0)
    both = matmul(stacked, factor)
    turned[...] = both[:, :lanes] + both[:, lanes:]

    pick = ones_where(iota((proj, proj), 1) == 2 * (iota((proj, proj), 0) % pairs) + iota((proj, proj), 0) // pairs)
    b, place = iota((proj, proj), 0), iota((proj, proj), 1)
    other, j = place // pairs, place % pairs
    even = ones_where(b == 2 * j + other)
    odd = ones_where(b == 2 * j + 1 - other)
    upper_rows = iota((proj, proj), 0) < pairs

    def arranged(part):
        picked = matmul(pick, part).astype(bf16)
        return jnp.where(upper_rows, matmul(picked, even), matmul(picked, odd)).astype(bf16)

    left_high, left_low = split(left[...])
    high, low = arranged(left_high), arranged(left_low)
    weights = jnp.concatenate([
        jnp.concatenate([high, high], axis=1),
        jnp.concatenate([low, jnp.zeros_like(low)], axis=1)], axis=0)
    group = 8
    first_half = iota((pairs, lanes * group), 1) % lanes < proj
    for start in range(0, rows, group):
        own = [turned[pl.ds(q, pairs, stride=rows), :] for q in range(start, start + group)]
        own_high, own_low = split(jnp.concatenate(own, axis=1))
        rolled_high, rolled_low = split(jnp.concatenate([pltpu.roll(v, proj, 1) for v in own], axis=1))
        value = matmul(weights, jnp.concatenate([own_high, rolled_high, own_low, rolled_low], axis=0))
        value = value[:proj] + value[proj:]
        value = jnp.where(first_half, value[:pairs], value[pairs:])
        for q in range(group):
            result[pl.ds((start + q) * pairs, pairs), :] = value[:, lanes * q:lanes * (q + 1)]
    for i in range(pairs):
        store(i, result[pl.ds(i, rows, stride=pairs), :].astype(bf16))


def kernel(query_ref, left_ref, right_ref, train_ref, out_ref, query, left_v, right_v, turned, result, held, heldx, train, trainx, acc, mine, stage_y, landed_y, stage_z, landed_z,
           stage_d, landed_d, in_sem, train_sem, trainx_sem, zs, zs2, zr, xs, xr, hs, hr, ps, pr,
           bs, bs2, br, axs, axr, ahs, ahr, aps, apr, ys, yr, ws, wr, ds, dr):
    g = lax.axis_index("layer")
    row = lax.axis_index("row")
    core = lax.rem(row, 2)
    z = lax.rem(row // 2, NZ)
    x = row // (2 * NZ)
    y = lax.rem(g, NY)
    zh = g // NY
    upper = z // 2
    zl = jnp.where(upper == 1, 3 - z, z)
    end = zl == 0
    inner = jnp.logical_not(end)
    right, left = lax.rem(x + 1, NX), lax.rem(x + NX - 1, NX)
    side = z + 1 - 2 * lax.rem(z, 2)
    across = 3 - z
    layers, rows, feat = query_ref.shape
    cols = held.shape[-1]
    few = rows // HALVES
    low, high = pl.ds(0, cols // 2), pl.ds(cols // 2, cols // 2)
    wide_low, wide_high = pl.ds(0, few), pl.ds(few, few)

    def device(xx, zz, cc):
        return (g, (xx * NZ + zz) * 2 + cc)

    def held_z(k):
        c = jnp.where(k == 0, zl, jnp.where(k == 1, 1 - zl, k))
        return jnp.where(upper == 1, 3 - c, c)

    def in_copies():
        return [pltpu.make_async_copy(src, dst, in_sem.at[n]) for n, (src, dst) in enumerate(
            ((query_ref, query), (left_ref, left_v), (right_ref, right_v)))]

    def train_copy(p):
        return pltpu.make_async_copy(
            train_ref.at[p, :, pl.ds(0, cols)], train.at[p], train_sem.at[p])

    def trainx_copy(q):
        return pltpu.make_async_copy(
            train_ref.at[q, :, pl.ds(feat - XCOLS, XCOLS)], trainx.at[q], trainx_sem.at[q])

    for copy in in_copies():
        copy.start()
    for p in range(layers):
        train_copy(p).start()
    for q in range(XPIECES):
        trainx_copy(q).start()

    barrier = pltpu.get_barrier_semaphore()

    def greet(target):
        pl.semaphore_signal(barrier, inc=1, device_id=target, device_id_type=MESH)

    greet(device(right, z, core))
    greet(device(left, z, core))
    greet(device(x, z, 1 - core))
    greet(device(x, side, core))
    greet(device(x, across, core))
    for j in range(1, NG):
        greet((lax.rem(g + j, NG), row))

    for copy in in_copies():
        copy.wait()
    tiles = cols // 128
    for layer in range(layers):
        def store(i, value):
            if i < tiles:
                for h in range(HALVES):
                    held[z, h * layers + layer, core, x, :, 128 * i:128 * (i + 1)] = value[h * few:(h + 1) * few]
            else:
                at = 128 * (i - tiles)
                heldx[z, layer, core, x, :, at:at + 128] = value

        precondition(query.at[layer], left_v.at[layer], right_v.at[layer], turned, result, store)

    pl.semaphore_wait(barrier, 5 + NG - 1)

    def remote(ref, send_sem, recv_sem, target):
        return pltpu.make_async_remote_copy(
            src_ref=ref, dst_ref=ref, send_sem=send_sem, recv_sem=recv_sem,
            device_id=target, device_id_type=MESH)

    def xdev(d):
        return device(right if d == 0 else left, z, core)

    def xsrc(d):
        return left if d == 0 else right

    def part(d):
        return low if d == 0 else high

    def wide_part(d):
        return wide_low if d == 0 else wide_high

    partner = device(x, z, 1 - core)

    def to_side(k, k_there, p):
        return remote(held.at[held_z(k), p, core, x], zs.at[k_there, p], zr.at[k_there, p], device(x, side, core))

    def to_across(k, k_there, p):
        return remote(held.at[held_z(k), p, core, x], zs2.at[k_there, p], zr.at[k_there, p], device(x, across, core))

    def to_x(k, p, d):
        return remote(held.at[held_z(k), p, core, x], xs.at[d, k, p], xr.at[d, k, p], xdev(d))

    def from_x(k, p, d):
        return remote(held.at[held_z(k), p, core, xsrc(d)], xs.at[d, k, p], xr.at[d, k, p], xdev(d))

    def relay(k, p, d):
        return remote(held.at[held_z(k), p, core, xsrc(d), :, part(d)], hs.at[d, k, p], hr.at[d, k, p], xdev(d))

    def to_partner(k, p):
        return remote(held.at[held_z(k), p, core], ps.at[k, p], pr.at[k, p], partner)

    def wide_to_x(q, d):
        return remote(heldx.at[z, q, core, x], axs.at[d, q], axr.at[d, q], xdev(d))

    def wide_from_x(q, d):
        return remote(heldx.at[z, q, core, xsrc(d)], axs.at[d, q], axr.at[d, q], xdev(d))

    def wide_relay(q, d):
        return remote(heldx.at[z, q, core, xsrc(d), wide_part(d)], ahs.at[d, q], ahr.at[d, q], xdev(d))

    def wide_to_side(k, k_there, q):
        return remote(heldx.at[held_z(k), q, core], bs.at[k_there, q], br.at[k_there, q], device(x, side, core))

    def wide_to_across(k, k_there, q):
        return remote(heldx.at[held_z(k), q, core], bs2.at[k_there, q], br.at[k_there, q], device(x, across, core))

    def wide_to_partner(k, q):
        return remote(heldx.at[held_z(k), q, core], aps.at[k, q], apr.at[k, q], partner)

    def to_y(k, h, t, b, dy):
        return pltpu.make_async_remote_copy(
            src_ref=stage_y.at[k, h, t], dst_ref=landed_y.at[b, h, y], send_sem=ys.at[k, h, t],
            recv_sem=yr.at[b, h, y], device_id=(zh * NY + dy, row), device_id_type=MESH)

    def from_y(b, h, sy):
        return pltpu.make_async_remote_copy(
            src_ref=stage_y.at[0, 0, 0], dst_ref=landed_y.at[b, h, sy], send_sem=ys.at[0, 0, 0],
            recv_sem=yr.at[b, h, sy], device_id=(zh * NY + sy, row), device_id_type=MESH)

    def to_z(b, h):
        return pltpu.make_async_remote_copy(
            src_ref=stage_z.at[b, h], dst_ref=landed_z.at[b, h], send_sem=ws.at[b, h], recv_sem=wr.at[b, h],
            device_id=((1 - zh) * NY + y, row), device_id_type=MESH)

    def to_owner(h, xx, owner):
        return pltpu.make_async_remote_copy(
            src_ref=stage_d.at[h, xx], dst_ref=landed_d.at[h, g], send_sem=ds.at[h, xx], recv_sem=dr.at[h, g],
            device_id=(owner, row), device_id_type=MESH)

    def from_member(h, src):
        return pltpu.make_async_remote_copy(
            src_ref=stage_d.at[0, 0], dst_ref=landed_d.at[h, src], send_sem=ds.at[0, 0], recv_sem=dr.at[h, src],
            device_id=(src, row), device_id_type=MESH)

    for q in range(XPIECES):
        for d in range(2):
            wide_to_x(q, d).start()
    for p in range(PIECES):
        to_side(0, 1, p).start()

        @pl.when(inner)
        def _():
            to_across(0, 2, p).start()

    def along_z(i):
        early = i - 3
        late = i - 8

        @pl.when(jnp.logical_and(inner, jnp.logical_and(early >= 0, early < PIECES)))
        def _():
            to_side(1, 1, early).wait_recv()
            to_across(1, 3, early).start()
            to_across(2, 2, early).wait_recv()
            to_side(2, 2, early).start()

        @pl.when(jnp.logical_and(inner, jnp.logical_and(late >= 0, late < PIECES)))
        def _():
            to_across(3, 3, late).wait_recv()
            to_side(3, 3, late).start()

    def wide(i):
        @pl.when(i == 1)
        def _():
            for q in range(XPIECES):
                for d in range(2):
                    wide_from_x(q, d).wait_recv()
                    wide_relay(q, d).start()

        @pl.when(i == 3)
        def _():
            for q in range(XPIECES):
                for d in range(2):
                    wide_relay(q, d).wait_recv()
                wide_to_side(0, 1, q).start()

                @pl.when(inner)
                def _():
                    wide_to_across(0, 2, q).start()

                wide_to_partner(0, q).start()

        @pl.when(i == 7)
        def _():
            for q in range(XPIECES):
                @pl.when(inner)
                def _():
                    wide_to_across(2, 2, q).wait_recv()
                    wide_to_side(2, 2, q).start()
                    wide_to_partner(2, q).start()

        @pl.when(i == 8)
        def _():
            for q in range(XPIECES):
                wide_to_side(1, 1, q).wait_recv()

                @pl.when(inner)
                def _():
                    wide_to_across(1, 3, q).start()

                wide_to_partner(1, q).start()

        @pl.when(jnp.logical_and(i == 12, inner))
        def _():
            for q in range(XPIECES):
                wide_to_across(3, 3, q).wait_recv()
                wide_to_side(3, 3, q).start()
                wide_to_partner(3, q).start()

        @pl.when(jnp.logical_and(i == 13, end))
        def _():
            for q in range(XPIECES):
                wide_to_side(2, 2, q).wait_recv()
                wide_to_partner(2, q).start()

        @pl.when(jnp.logical_and(i == 17, end))
        def _():
            for q in range(XPIECES):
                wide_to_side(3, 3, q).wait_recv()
                wide_to_partner(3, q).start()

    def sums_of(xx):
        return [acc[pl.ds((c * NX + xx) * few, few), :] for c in range(2)]

    def send_sums(k, h):
        zz = held_z(k)
        b = lax.rem(zz, 2)

        @pl.when(k < NZ - 1)
        def _():
            for t in range(2):
                dy = 2 * t + zz // 2

                @pl.when(dy == y)
                def _():
                    for u in range(2):
                        for c, value in enumerate(sums_of(2 * u + t)):
                            mine[b, h, u, pl.ds(c * few, few), :] = value

                @pl.when(dy != y)
                def _():
                    for u in range(2):
                        for c, value in enumerate(sums_of(2 * u + t)):
                            stage_y[k, h, t, u, pl.ds(c * few, few), :] = value.astype(jnp.bfloat16)
                    to_y(k, h, t, b, dy).start()

        @pl.when(k == NZ - 1)
        def _():
            for n in range(NX):
                xx = lax.rem(n + 2 * (1 - zh), NX)
                owner = 2 * xx + zz // 2
                pieces = [acc[pl.ds(pl.multiple_of((c * NX + xx) * few, few), few), :] for c in range(2)]

                @pl.when(owner == g)
                def _():
                    for c, value in enumerate(pieces):
                        mine[b, h, zh, pl.ds(c * few, few), :] = value

                @pl.when(owner != g)
                def _():
                    for c, value in enumerate(pieces):
                        stage_d[h, xx, pl.ds(c * few, few), :] = value.astype(jnp.bfloat16)
                    to_owner(h, xx, owner).start()

    def reduce_y(i):
        n = i - AT_SUM
        k, h = n // PIECES, lax.rem(n + PIECES, PIECES) // layers

        @pl.when(jnp.logical_and(n >= 0, jnp.logical_and(lax.rem(n + PIECES, layers) == 0, k < NZ - 1)))
        def _():
            zz = held_z(k)
            b = lax.rem(zz, 2)

            @pl.when(zz // 2 == lax.rem(y, 2))
            def _():
                for j in range(1, NY):
                    from_y(b, h, lax.rem(y + j, NY)).wait_recv()

                def total(u):
                    value = mine[b, h, u]
                    for j in range(1, NY):
                        value = value + landed_y[b, h, lax.rem(y + j, NY), u].astype(jnp.float32)
                    return value

                stage_z[b, h] = total(1 - zh).astype(jnp.bfloat16)
                to_z(b, h).start()
                mine[b, h, zh] = total(zh)

    def step(i, carry):
        along_z(i)
        wide(i)

        @pl.when(i < STEPS)
        def _():
            k, p = i // PIECES, lax.rem(i, PIECES)

            @pl.when(jnp.logical_and(end, k > 0))
            def _():
                to_side(k, k, p).wait_recv()

            to_x(k, p, 0).start()
            to_x(k, p, 1).start()

        @pl.when(jnp.logical_and(i >= AT_B, i < STEPS + AT_B))
        def _():
            s = i - AT_B
            k, p = s // PIECES, lax.rem(s, PIECES)
            from_x(k, p, 0).wait_recv()
            relay(k, p, 0).start()
            from_x(k, p, 1).wait_recv()
            relay(k, p, 1).start()

        @pl.when(jnp.logical_and(i >= AT_C, i < STEPS + AT_C))
        def _():
            s = i - AT_C
            k, p = s // PIECES, lax.rem(s, PIECES)
            relay(k, p, 0).wait_recv()
            relay(k, p, 1).wait_recv()
            to_partner(k, p).start()

        @pl.when(i >= AT_D)
        def _():
            s = i - AT_D
            k, p = s // PIECES, lax.rem(s, PIECES)

            h, layer = p // layers, lax.rem(p, layers)

            def product(lhs, rhs):
                return lax.dot_general(lhs.reshape(2 * NX * few, lhs.shape[-1]), rhs, (((1,), (1,)), ((), ())),
                                       preferred_element_type=jnp.float32)

            @pl.when(s == 0)
            def _():
                for q in range(XPIECES):
                    trainx_copy(q).wait()

            @pl.when(s < layers)
            def _():
                pltpu.make_async_copy(train.at[layer], train.at[layer], train_sem.at[layer]).wait()

            to_partner(k, p).wait_recv()
            term = product(held[held_z(k), p], train[layer])

            @pl.when(layer == 0)
            def _():
                acc[...] = term

            @pl.when(layer > 0)
            def _():
                acc[...] += term

            @pl.when(jnp.logical_or(p == layers - 1, p == layers))
            def _():
                for q in range(XPIECES):
                    @pl.when(h == 0)
                    def _():
                        wide_to_partner(k, q).wait_recv()

                    acc[...] += product(heldx[held_z(k), q, :, :, pl.ds(pl.multiple_of(h * few, few), few), :], trainx[q])

            @pl.when(layer == layers - 1)
            def _():
                send_sums(k, h)

        reduce_y(i)
        return carry

    lax.fori_loop(0, STEPS + AT_D, step, 0)

    late_owner = lax.rem(y, 2) != upper
    last_b = lax.rem(held_z(NZ - 1), 2)
    for h in range(HALVES):
        for b in range(2):
            direct = jnp.logical_and(late_owner, last_b == b)

            def put(value):
                for c in range(2):
                    out_ref[pl.ds(b * 2 * rows + c * rows + h * few, few), :] = value[c * few:(c + 1) * few]

            @pl.when(jnp.logical_not(direct))
            def _():
                to_z(b, h).wait_recv()
                put(mine[b, h, zh] + landed_z[b, h].astype(jnp.float32))

            @pl.when(direct)
            def _():
                value = mine[b, h, zh]
                for j in range(1, NG):
                    src = lax.rem(g + j, NG)
                    from_member(h, src).wait_recv()
                    value = value + landed_d[h, src].astype(jnp.float32)
                put(value)

    def drain(s, carry):
        k, p = s // PIECES, lax.rem(s, PIECES)
        for d in range(2):
            to_x(k, p, d).wait_send()
            relay(k, p, d).wait_send()
        to_partner(k, p).wait_send()

        @pl.when(k == 0)
        def _():
            to_side(0, 1, p).wait_send()

        @pl.when(inner)
        def _():
            @pl.when(k == 0)
            def _():
                to_across(0, 2, p).wait_send()

            @pl.when(k == 1)
            def _():
                to_across(1, 3, p).wait_send()

            @pl.when(k >= 2)
            def _():
                to_side(k, k, p).wait_send()

        return carry

    lax.fori_loop(0, STEPS, drain, 0)
    for q in range(XPIECES):
        for d in range(2):
            wide_to_x(q, d).wait_send()
            wide_relay(q, d).wait_send()
        wide_to_side(0, 1, q).wait_send()
        for k in range(NZ):
            wide_to_partner(k, q).wait_send()

        @pl.when(inner)
        def _():
            wide_to_across(0, 2, q).wait_send()
            wide_to_across(1, 3, q).wait_send()
            wide_to_side(2, 2, q).wait_send()
            wide_to_side(3, 3, q).wait_send()

    for h in range(HALVES):
        for k in range(NZ - 1):
            zz = held_z(k)
            for t in range(2):
                @pl.when(2 * t + zz // 2 != y)
                def _():
                    to_y(k, h, t, 0, 0).wait_send()

        for b in range(2):
            @pl.when(jnp.logical_not(jnp.logical_and(late_owner, last_b == b)))
            def _():
                to_z(b, h).wait_send()

        for xx in range(NX):
            @pl.when(2 * xx + held_z(NZ - 1) // 2 != g)
            def _():
                to_owner(h, xx, 0).wait_send()


def on_device(query_grads, train_grads, left_inverse, right_inverse):
    layers, rows, feat = query_grads.shape
    proj = left_inverse.shape[1]
    train_rows = train_grads.shape[1]
    cols = feat - XCOLS
    few = rows // HALVES
    block = NX * NZ * 2 * rows // NG
    dma = pltpu.SemaphoreType.DMA
    bf16, f32 = jnp.bfloat16, jnp.float32
    return pl.pallas_call(
        kernel,
        out_shape=pltpu.VMEM((block, train_rows), f32),
        in_specs=[pl.BlockSpec(memory_space=pl.ANY)] * 4,
        out_specs=pl.BlockSpec(memory_space=pltpu.VMEM),
        scratch_shapes=[
            pltpu.VMEM((layers, rows, feat), bf16),
            pltpu.VMEM((layers, proj, proj), f32),
            pltpu.VMEM((layers, proj, proj), f32),
            pltpu.VMEM((rows * proj // 2, 2 * proj), f32),
            pltpu.VMEM((rows * proj // 2, 2 * proj), f32),
            pltpu.VMEM((NZ, PIECES, 2, NX, few, cols), bf16),
            pltpu.VMEM((NZ, XPIECES, 2, NX, rows, XCOLS), bf16),
            pltpu.VMEM((layers, train_rows, cols), bf16),
            pltpu.VMEM((XPIECES, train_rows, XCOLS), bf16),
            pltpu.VMEM((2 * NX * few, train_rows), f32),
            pltpu.VMEM((2, HALVES, 2, 2 * few, train_rows), f32),
            pltpu.VMEM((NZ - 1, HALVES, 2, 2, 2 * few, train_rows), bf16),
            pltpu.VMEM((2, HALVES, NY, 2, 2 * few, train_rows), bf16),
            pltpu.VMEM((2, HALVES, 2 * few, train_rows), bf16),
            pltpu.VMEM((2, HALVES, 2 * few, train_rows), bf16),
            pltpu.VMEM((HALVES, NX, 2 * few, train_rows), bf16),
            pltpu.VMEM((HALVES, NG, 2 * few, train_rows), bf16),
            dma((3,)), dma((layers,)), dma((XPIECES,)),
            dma((NZ, PIECES)), dma((NZ, PIECES)), dma((NZ, PIECES)),
            dma((2, NZ, PIECES)), dma((2, NZ, PIECES)), dma((2, NZ, PIECES)), dma((2, NZ, PIECES)),
            dma((NZ, PIECES)), dma((NZ, PIECES)),
            dma((NZ, XPIECES)), dma((NZ, XPIECES)), dma((NZ, XPIECES)),
            dma((2, XPIECES)), dma((2, XPIECES)), dma((2, XPIECES)), dma((2, XPIECES)),
            dma((NZ, XPIECES)), dma((NZ, XPIECES)),
            dma((NZ - 1, HALVES, 2)), dma((2, HALVES, NY)), dma((2, HALVES)), dma((2, HALVES)),
            dma((HALVES, NX)), dma((HALVES, NG)),
        ],
        compiler_params=pltpu.CompilerParams(
            collective_id=0, has_side_effects=True, vmem_limit_bytes=60 * 1024 * 1024),
    )(query_grads, left_inverse, right_inverse, train_grads)


def solution(mesh):
    placed = (
        P("layer", "row", None),
        P("layer", "row", None),
        P("layer", None, None),
        P("layer", None, None),
    )
    return jax.shard_map(
        on_device, mesh=mesh, in_specs=placed, out_specs=P("layer", "row"), check_vma=False
    )
```

```python
import jax
import jax.numpy as jnp
from jax import lax
from jax.experimental import pallas as pl
from jax.experimental.pallas import tpu as pltpu
from jax.sharding import PartitionSpec as P

MESH = pl.DeviceIdType.MESH
NX, NY, NZ, NG = 4, 4, 4, 8
PIECES = 4
STEPS = NZ * PIECES
XPIECES = 2
XCOLS = 768
HALVES = 2
AT_B, AT_C, AT_D, AT_SUM = 2, 4, 5, 8


def split(value):
    high = value.astype(jnp.bfloat16)
    return high, (value - high.astype(jnp.float32)).astype(jnp.bfloat16)


def matmul(a, b):
    return jnp.dot(a, b, preferred_element_type=jnp.float32)


def precondition(query, left, right, turned, result, store):
    rows, feat = query.shape
    proj = left.shape[0]
    pairs = proj // 2
    lanes = 2 * proj
    bf16, f32 = jnp.bfloat16, jnp.float32

    def iota(shape, axis):
        return lax.broadcasted_iota(jnp.int32, shape, axis)

    def ones_where(mask):
        return jnp.where(mask, 1.0, 0.0).astype(bf16)

    twice = ones_where(iota((proj, lanes), 1) % proj == iota((proj, lanes), 0))
    same_half = iota((lanes, lanes), 0) // proj == iota((lanes, lanes), 1) // proj

    def block_diagonal(part):
        wide = matmul(part, twice)
        return jnp.where(same_half, jnp.concatenate([wide, wide], axis=0), 0.0).astype(bf16)

    right_high, right_low = split(right[...])
    factor = jnp.concatenate([block_diagonal(right_high), block_diagonal(right_low)], axis=1)
    stacked = jnp.concatenate([query[:, lanes * j:lanes * (j + 1)] for j in range(pairs)], axis=0)
    both = matmul(stacked, factor)
    turned[...] = both[:, :lanes] + both[:, lanes:]

    pick = ones_where(iota((proj, proj), 1) == 2 * (iota((proj, proj), 0) % pairs) + iota((proj, proj), 0) // pairs)
    b, place = iota((proj, proj), 0), iota((proj, proj), 1)
    other, j = place // pairs, place % pairs
    even = ones_where(b == 2 * j + other)
    odd = ones_where(b == 2 * j + 1 - other)
    upper_rows = iota((proj, proj), 0) < pairs

    def arranged(part):
        picked = matmul(pick, part).astype(bf16)
        return jnp.where(upper_rows, matmul(picked, even), matmul(picked, odd)).astype(bf16)

    left_high, left_low = split(left[...])
    high, low = arranged(left_high), arranged(left_low)
    weights = jnp.concatenate([
        jnp.concatenate([high, high], axis=1),
        jnp.concatenate([low, jnp.zeros_like(low)], axis=1)], axis=0)
    group = 8
    first_half = iota((pairs, lanes * group), 1) % lanes < proj
    for start in range(0, rows, group):
        own = [turned[pl.ds(q, pairs, stride=rows), :] for q in range(start, start + group)]
        own_high, own_low = split(jnp.concatenate(own, axis=1))
        rolled_high, rolled_low = split(jnp.concatenate([pltpu.roll(v, proj, 1) for v in own], axis=1))
        value = matmul(weights, jnp.concatenate([own_high, rolled_high, own_low, rolled_low], axis=0))
        value = value[:proj] + value[proj:]
        value = jnp.where(first_half, value[:pairs], value[pairs:])
        for q in range(group):
            result[pl.ds((start + q) * pairs, pairs), :] = value[:, lanes * q:lanes * (q + 1)]
    for i in range(pairs):
        store(i, result[pl.ds(i, rows, stride=pairs), :].astype(bf16))


def kernel(query_ref, left_ref, right_ref, train_ref, out_ref, query, left_v, right_v, turned, result, held, heldx, train, trainx, acc, mine, stage_y, landed_y, stage_z, landed_z,
           stage_d, landed_d, in_sem, train_sem, trainx_sem, zs, zs2, zr, xs, xr, hs, hr, ps, pr,
           bs, bs2, br, axs, axr, ahs, ahr, aps, apr, ys, yr, ws, wr, ds, dr):
    g = lax.axis_index("layer")
    row = lax.axis_index("row")
    core = lax.rem(row, 2)
    z = lax.rem(row // 2, NZ)
    x = row // (2 * NZ)
    y = lax.rem(g, NY)
    zh = g // NY
    upper = z // 2
    zl = jnp.where(upper == 1, 3 - z, z)
    end = zl == 0
    inner = jnp.logical_not(end)
    right, left = lax.rem(x + 1, NX), lax.rem(x + NX - 1, NX)
    side = z + 1 - 2 * lax.rem(z, 2)
    across = 3 - z
    layers, rows, feat = query_ref.shape
    cols = held.shape[-1]
    few = rows // HALVES
    low, high = pl.ds(0, cols // 2), pl.ds(cols // 2, cols // 2)
    wide_low, wide_high = pl.ds(0, few), pl.ds(few, few)

    def device(xx, zz, cc):
        return (g, (xx * NZ + zz) * 2 + cc)

    def held_z(k):
        c = jnp.where(k == 0, zl, jnp.where(k == 1, 1 - zl, k))
        return jnp.where(upper == 1, 3 - c, c)

    def in_copies():
        return [pltpu.make_async_copy(src, dst, in_sem.at[n]) for n, (src, dst) in enumerate(
            ((query_ref, query), (left_ref, left_v), (right_ref, right_v)))]

    def train_copy(p):
        return pltpu.make_async_copy(
            train_ref.at[p, :, pl.ds(0, cols)], train.at[p], train_sem.at[p])

    def trainx_copy(q):
        return pltpu.make_async_copy(
            train_ref.at[q, :, pl.ds(feat - XCOLS, XCOLS)], trainx.at[q], trainx_sem.at[q])

    for copy in in_copies():
        copy.start()
    for p in range(layers):
        train_copy(p).start()
    for q in range(XPIECES):
        trainx_copy(q).start()

    barrier = pltpu.get_barrier_semaphore()

    def greet(target):
        pl.semaphore_signal(barrier, inc=1, device_id=target, device_id_type=MESH)

    greet(device(right, z, core))
    greet(device(left, z, core))
    greet(device(x, z, 1 - core))
    greet(device(x, side, core))
    greet(device(x, across, core))
    for j in range(1, NG):
        greet((lax.rem(g + j, NG), row))

    for copy in in_copies():
        copy.wait()
    tiles = cols // 128
    for layer in range(layers):
        def store(i, value):
            if i < tiles:
                for h in range(HALVES):
                    held[z, h * layers + layer, core, x, :, 128 * i:128 * (i + 1)] = value[h * few:(h + 1) * few]
            else:
                at = 128 * (i - tiles)
                heldx[z, layer, core, x, :, at:at + 128] = value

        precondition(query.at[layer], left_v.at[layer], right_v.at[layer], turned, result, store)

    pl.semaphore_wait(barrier, 5 + NG - 1)

    def remote(ref, send_sem, recv_sem, target):
        return pltpu.make_async_remote_copy(
            src_ref=ref, dst_ref=ref, send_sem=send_sem, recv_sem=recv_sem,
            device_id=target, device_id_type=MESH)

    def xdev(d):
        return device(right if d == 0 else left, z, core)

    def xsrc(d):
        return left if d == 0 else right

    def part(d):
        return low if d == 0 else high

    def wide_part(d):
        return wide_low if d == 0 else wide_high

    partner = device(x, z, 1 - core)

    def to_side(k, k_there, p):
        return remote(held.at[held_z(k), p, core, x], zs.at[k_there, p], zr.at[k_there, p], device(x, side, core))

    def to_across(k, k_there, p):
        return remote(held.at[held_z(k), p, core, x], zs2.at[k_there, p], zr.at[k_there, p], device(x, across, core))

    def to_x(k, p, d):
        return remote(held.at[held_z(k), p, core, x], xs.at[d, k, p], xr.at[d, k, p], xdev(d))

    def from_x(k, p, d):
        return remote(held.at[held_z(k), p, core, xsrc(d)], xs.at[d, k, p], xr.at[d, k, p], xdev(d))

    def relay(k, p, d):
        return remote(held.at[held_z(k), p, core, xsrc(d), :, part(d)], hs.at[d, k, p], hr.at[d, k, p], xdev(d))

    def to_partner(k, p):
        return remote(held.at[held_z(k), p, core], ps.at[k, p], pr.at[k, p], partner)

    def wide_to_x(q, d):
        return remote(heldx.at[z, q, core, x], axs.at[d, q], axr.at[d, q], xdev(d))

    def wide_from_x(q, d):
        return remote(heldx.at[z, q, core, xsrc(d)], axs.at[d, q], axr.at[d, q], xdev(d))

    def wide_relay(q, d):
        return remote(heldx.at[z, q, core, xsrc(d), wide_part(d)], ahs.at[d, q], ahr.at[d, q], xdev(d))

    def wide_to_side(k, k_there, q):
        return remote(heldx.at[held_z(k), q, core], bs.at[k_there, q], br.at[k_there, q], device(x, side, core))

    def wide_to_across(k, k_there, q):
        return remote(heldx.at[held_z(k), q, core], bs2.at[k_there, q], br.at[k_there, q], device(x, across, core))

    def wide_to_partner(k, q):
        return remote(heldx.at[held_z(k), q, core], aps.at[k, q], apr.at[k, q], partner)

    def to_y(k, h, t, b, dy):
        return pltpu.make_async_remote_copy(
            src_ref=stage_y.at[k, h, t], dst_ref=landed_y.at[b, h, y], send_sem=ys.at[k, h, t],
            recv_sem=yr.at[b, h, y], device_id=(zh * NY + dy, row), device_id_type=MESH)

    def from_y(b, h, sy):
        return pltpu.make_async_remote_copy(
            src_ref=stage_y.at[0, 0, 0], dst_ref=landed_y.at[b, h, sy], send_sem=ys.at[0, 0, 0],
            recv_sem=yr.at[b, h, sy], device_id=(zh * NY + sy, row), device_id_type=MESH)

    def to_z(b, h):
        return pltpu.make_async_remote_copy(
            src_ref=stage_z.at[b, h], dst_ref=landed_z.at[b, h], send_sem=ws.at[b, h], recv_sem=wr.at[b, h],
            device_id=((1 - zh) * NY + y, row), device_id_type=MESH)

    def to_owner(h, xx, owner):
        return pltpu.make_async_remote_copy(
            src_ref=stage_d.at[h, xx], dst_ref=landed_d.at[h, g], send_sem=ds.at[h, xx], recv_sem=dr.at[h, g],
            device_id=(owner, row), device_id_type=MESH)

    def from_member(h, src):
        return pltpu.make_async_remote_copy(
            src_ref=stage_d.at[0, 0], dst_ref=landed_d.at[h, src], send_sem=ds.at[0, 0], recv_sem=dr.at[h, src],
            device_id=(src, row), device_id_type=MESH)

    for q in range(XPIECES):
        for d in range(2):
            wide_to_x(q, d).start()
    for p in range(PIECES):
        to_side(0, 1, p).start()

        @pl.when(inner)
        def _():
            to_across(0, 2, p).start()

    def along_z(i):
        early = i - 3
        late = i - 8

        @pl.when(jnp.logical_and(inner, jnp.logical_and(early >= 0, early < PIECES)))
        def _():
            to_side(1, 1, early).wait_recv()
            to_across(1, 3, early).start()
            to_across(2, 2, early).wait_recv()
            to_side(2, 2, early).start()

        @pl.when(jnp.logical_and(inner, jnp.logical_and(late >= 0, late < PIECES)))
        def _():
            to_across(3, 3, late).wait_recv()
            to_side(3, 3, late).start()

    def wide(i):
        @pl.when(i == 1)
        def _():
            for q in range(XPIECES):
                for d in range(2):
                    wide_from_x(q, d).wait_recv()
                    wide_relay(q, d).start()

        @pl.when(i == 3)
        def _():
            for q in range(XPIECES):
                for d in range(2):
                    wide_relay(q, d).wait_recv()
                wide_to_side(0, 1, q).start()

                @pl.when(inner)
                def _():
                    wide_to_across(0, 2, q).start()

                wide_to_partner(0, q).start()

        @pl.when(i == 7)
        def _():
            for q in range(XPIECES):
                @pl.when(inner)
                def _():
                    wide_to_across(2, 2, q).wait_recv()
                    wide_to_side(2, 2, q).start()
                    wide_to_partner(2, q).start()

        @pl.when(i == 8)
        def _():
            for q in range(XPIECES):
                wide_to_side(1, 1, q).wait_recv()

                @pl.when(inner)
                def _():
                    wide_to_across(1, 3, q).start()

                wide_to_partner(1, q).start()

        @pl.when(jnp.logical_and(i == 12, inner))
        def _():
            for q in range(XPIECES):
                wide_to_across(3, 3, q).wait_recv()
                wide_to_side(3, 3, q).start()
                wide_to_partner(3, q).start()

        @pl.when(jnp.logical_and(i == 13, end))
        def _():
            for q in range(XPIECES):
                wide_to_side(2, 2, q).wait_recv()
                wide_to_partner(2, q).start()

        @pl.when(jnp.logical_and(i == 17, end))
        def _():
            for q in range(XPIECES):
                wide_to_side(3, 3, q).wait_recv()
                wide_to_partner(3, q).start()

    def sums_of(xx):
        return [acc[pl.ds((c * NX + xx) * few, few), :] for c in range(2)]

    def send_sums(k, h):
        zz = held_z(k)
        b = lax.rem(zz, 2)

        @pl.when(k < NZ - 1)
        def _():
            for t in range(2):
                dy = 2 * t + zz // 2

                @pl.when(dy == y)
                def _():
                    for u in range(2):
                        for c, value in enumerate(sums_of(2 * u + t)):
                            mine[b, h, u, pl.ds(c * few, few), :] = value

                @pl.when(dy != y)
                def _():
                    for u in range(2):
                        for c, value in enumerate(sums_of(2 * u + t)):
                            stage_y[k, h, t, u, pl.ds(c * few, few), :] = value.astype(jnp.bfloat16)
                    to_y(k, h, t, b, dy).start()

        @pl.when(k == NZ - 1)
        def _():
            for n in range(NX):
                xx = lax.rem(n + 2 * (1 - zh), NX)
                owner = 2 * xx + zz // 2
                pieces = [acc[pl.ds(pl.multiple_of((c * NX + xx) * few, few), few), :] for c in range(2)]

                @pl.when(owner == g)
                def _():
                    for c, value in enumerate(pieces):
                        mine[b, h, zh, pl.ds(c * few, few), :] = value

                @pl.when(owner != g)
                def _():
                    for c, value in enumerate(pieces):
                        stage_d[h, xx, pl.ds(c * few, few), :] = value.astype(jnp.bfloat16)
                    to_owner(h, xx, owner).start()

    def reduce_y(i):
        n = i - AT_SUM
        k, h = n // PIECES, lax.rem(n + PIECES, PIECES) // layers

        @pl.when(jnp.logical_and(n >= 0, jnp.logical_and(lax.rem(n + PIECES, layers) == 0, k < NZ - 1)))
        def _():
            zz = held_z(k)
            b = lax.rem(zz, 2)

            @pl.when(zz // 2 == lax.rem(y, 2))
            def _():
                for j in range(1, NY):
                    from_y(b, h, lax.rem(y + j, NY)).wait_recv()

                def total(u):
                    value = mine[b, h, u]
                    for j in range(1, NY):
                        value = value + landed_y[b, h, lax.rem(y + j, NY), u].astype(jnp.float32)
                    return value

                stage_z[b, h] = total(1 - zh).astype(jnp.bfloat16)
                to_z(b, h).start()
                mine[b, h, zh] = total(zh)

    def step(i, carry):
        along_z(i)
        wide(i)

        @pl.when(i < STEPS)
        def _():
            k, p = i // PIECES, lax.rem(i, PIECES)

            @pl.when(jnp.logical_and(end, k > 0))
            def _():
                to_side(k, k, p).wait_recv()

            to_x(k, p, 0).start()
            to_x(k, p, 1).start()

        @pl.when(jnp.logical_and(i >= AT_B, i < STEPS + AT_B))
        def _():
            s = i - AT_B
            k, p = s // PIECES, lax.rem(s, PIECES)
            from_x(k, p, 0).wait_recv()
            relay(k, p, 0).start()
            from_x(k, p, 1).wait_recv()
            relay(k, p, 1).start()

        @pl.when(jnp.logical_and(i >= AT_C, i < STEPS + AT_C))
        def _():
            s = i - AT_C
            k, p = s // PIECES, lax.rem(s, PIECES)
            relay(k, p, 0).wait_recv()
            relay(k, p, 1).wait_recv()
            to_partner(k, p).start()

        @pl.when(i >= AT_D)
        def _():
            s = i - AT_D
            k, p = s // PIECES, lax.rem(s, PIECES)

            h, layer = p // layers, lax.rem(p, layers)

            def product(lhs, rhs):
                return lax.dot_general(lhs.reshape(2 * NX * few, lhs.shape[-1]), rhs, (((1,), (1,)), ((), ())),
                                       preferred_element_type=jnp.float32)

            @pl.when(s == 0)
            def _():
                for q in range(XPIECES):
                    trainx_copy(q).wait()

            @pl.when(s < layers)
            def _():
                pltpu.make_async_copy(train.at[layer], train.at[layer], train_sem.at[layer]).wait()

            to_partner(k, p).wait_recv()
            term = product(held[held_z(k), p], train[layer])

            @pl.when(layer == 0)
            def _():
                acc[...] = term

            @pl.when(layer > 0)
            def _():
                acc[...] += term

            @pl.when(jnp.logical_or(p == layers - 1, p == layers))
            def _():
                for q in range(XPIECES):
                    @pl.when(h == 0)
                    def _():
                        wide_to_partner(k, q).wait_recv()

                    acc[...] += product(heldx[held_z(k), q, :, :, pl.ds(pl.multiple_of(h * few, few), few), :], trainx[q])

            @pl.when(layer == layers - 1)
            def _():
                send_sums(k, h)

        reduce_y(i)
        return carry

    lax.fori_loop(0, STEPS + AT_D, step, 0)

    def drain(s, carry):
        k, p = s // PIECES, lax.rem(s, PIECES)
        for d in range(2):
            to_x(k, p, d).wait_send()
            relay(k, p, d).wait_send()
        to_partner(k, p).wait_send()

        @pl.when(k == 0)
        def _():
            to_side(0, 1, p).wait_send()

        @pl.when(inner)
        def _():
            @pl.when(k == 0)
            def _():
                to_across(0, 2, p).wait_send()

            @pl.when(k == 1)
            def _():
                to_across(1, 3, p).wait_send()

            @pl.when(k >= 2)
            def _():
                to_side(k, k, p).wait_send()

        return carry

    lax.fori_loop(0, STEPS, drain, 0)
    for q in range(XPIECES):
        for d in range(2):
            wide_to_x(q, d).wait_send()
            wide_relay(q, d).wait_send()
        wide_to_side(0, 1, q).wait_send()
        for k in range(NZ):
            wide_to_partner(k, q).wait_send()

        @pl.when(inner)
        def _():
            wide_to_across(0, 2, q).wait_send()
            wide_to_across(1, 3, q).wait_send()
            wide_to_side(2, 2, q).wait_send()
            wide_to_side(3, 3, q).wait_send()

    for h in range(HALVES):
        for k in range(NZ - 1):
            zz = held_z(k)
            for t in range(2):
                @pl.when(2 * t + zz // 2 != y)
                def _():
                    to_y(k, h, t, 0, 0).wait_send()

    late_owner = lax.rem(y, 2) != upper
    last_b = lax.rem(held_z(NZ - 1), 2)
    for h in range(HALVES):
        for b in range(2):
            direct = jnp.logical_and(late_owner, last_b == b)

            def put(value):
                for c in range(2):
                    out_ref[pl.ds(b * 2 * rows + c * rows + h * few, few), :] = value[c * few:(c + 1) * few]

            @pl.when(jnp.logical_not(direct))
            def _():
                to_z(b, h).wait_recv()
                put(mine[b, h, zh] + landed_z[b, h].astype(jnp.float32))

            @pl.when(direct)
            def _():
                value = mine[b, h, zh]
                for j in range(1, NG):
                    src = lax.rem(g + j, NG)
                    from_member(h, src).wait_recv()
                    value = value + landed_d[h, src].astype(jnp.float32)
                put(value)

    for h in range(HALVES):
        for b in range(2):
            @pl.when(jnp.logical_not(jnp.logical_and(late_owner, last_b == b)))
            def _():
                to_z(b, h).wait_send()

        for xx in range(NX):
            @pl.when(2 * xx + held_z(NZ - 1) // 2 != g)
            def _():
                to_owner(h, xx, 0).wait_send()


def on_device(query_grads, train_grads, left_inverse, right_inverse):
    layers, rows, feat = query_grads.shape
    proj = left_inverse.shape[1]
    train_rows = train_grads.shape[1]
    cols = feat - XCOLS
    few = rows // HALVES
    block = NX * NZ * 2 * rows // NG
    dma = pltpu.SemaphoreType.DMA
    bf16, f32 = jnp.bfloat16, jnp.float32
    return pl.pallas_call(
        kernel,
        out_shape=pltpu.VMEM((block, train_rows), f32),
        in_specs=[pl.BlockSpec(memory_space=pl.ANY)] * 4,
        out_specs=pl.BlockSpec(memory_space=pltpu.VMEM),
        scratch_shapes=[
            pltpu.VMEM((layers, rows, feat), bf16),
            pltpu.VMEM((layers, proj, proj), f32),
            pltpu.VMEM((layers, proj, proj), f32),
            pltpu.VMEM((rows * proj // 2, 2 * proj), f32),
            pltpu.VMEM((rows * proj // 2, 2 * proj), f32),
            pltpu.VMEM((NZ, PIECES, 2, NX, few, cols), bf16),
            pltpu.VMEM((NZ, XPIECES, 2, NX, rows, XCOLS), bf16),
            pltpu.VMEM((layers, train_rows, cols), bf16),
            pltpu.VMEM((XPIECES, train_rows, XCOLS), bf16),
            pltpu.VMEM((2 * NX * few, train_rows), f32),
            pltpu.VMEM((2, HALVES, 2, 2 * few, train_rows), f32),
            pltpu.VMEM((NZ - 1, HALVES, 2, 2, 2 * few, train_rows), bf16),
            pltpu.VMEM((2, HALVES, NY, 2, 2 * few, train_rows), bf16),
            pltpu.VMEM((2, HALVES, 2 * few, train_rows), bf16),
            pltpu.VMEM((2, HALVES, 2 * few, train_rows), bf16),
            pltpu.VMEM((HALVES, NX, 2 * few, train_rows), bf16),
            pltpu.VMEM((HALVES, NG, 2 * few, train_rows), bf16),
            dma((3,)), dma((layers,)), dma((XPIECES,)),
            dma((NZ, PIECES)), dma((NZ, PIECES)), dma((NZ, PIECES)),
            dma((2, NZ, PIECES)), dma((2, NZ, PIECES)), dma((2, NZ, PIECES)), dma((2, NZ, PIECES)),
            dma((NZ, PIECES)), dma((NZ, PIECES)),
            dma((NZ, XPIECES)), dma((NZ, XPIECES)), dma((NZ, XPIECES)),
            dma((2, XPIECES)), dma((2, XPIECES)), dma((2, XPIECES)), dma((2, XPIECES)),
            dma((NZ, XPIECES)), dma((NZ, XPIECES)),
            dma((NZ - 1, HALVES, 2)), dma((2, HALVES, NY)), dma((2, HALVES)), dma((2, HALVES)),
            dma((HALVES, NX)), dma((HALVES, NG)),
        ],
        compiler_params=pltpu.CompilerParams(
            collective_id=0, has_side_effects=True, vmem_limit_bytes=60 * 1024 * 1024),
    )(query_grads, left_inverse, right_inverse, train_grads)


def solution(mesh):
    placed = (
        P("layer", "row", None),
        P("layer", "row", None),
        P("layer", None, None),
        P("layer", None, None),
    )
    return jax.shard_map(
        on_device, mesh=mesh, in_specs=placed, out_specs=P("layer", "row"), check_vma=False
    )
```

```python
import jax
import jax.numpy as jnp
from jax import lax
from jax.experimental import pallas as pl
from jax.experimental.pallas import tpu as pltpu
from jax.sharding import PartitionSpec as P

MESH = pl.DeviceIdType.MESH
NX, NY, NZ, NG = 4, 4, 4, 8
PIECES = 4
STEPS = NZ * PIECES
XPIECES = 2
XCOLS = 768
HALVES = 2
AT_B, AT_C, AT_D, AT_SUM = 2, 4, 5, 8


def split(value):
    high = value.astype(jnp.bfloat16)
    return high, (value - high.astype(jnp.float32)).astype(jnp.bfloat16)


def matmul(a, b):
    return jnp.dot(a, b, preferred_element_type=jnp.float32)


def precondition(query, left, right, turned, result, store):
    rows, feat = query.shape
    proj = left.shape[0]
    pairs = proj // 2
    lanes = 2 * proj
    bf16, f32 = jnp.bfloat16, jnp.float32

    def iota(shape, axis):
        return lax.broadcasted_iota(jnp.int32, shape, axis)

    def ones_where(mask):
        return jnp.where(mask, 1.0, 0.0).astype(bf16)

    twice = ones_where(iota((proj, lanes), 1) % proj == iota((proj, lanes), 0))
    same_half = iota((lanes, lanes), 0) // proj == iota((lanes, lanes), 1) // proj

    def block_diagonal(part):
        wide = matmul(part, twice)
        return jnp.where(same_half, jnp.concatenate([wide, wide], axis=0), 0.0).astype(bf16)

    right_high, right_low = split(right[...])
    factor = jnp.concatenate([block_diagonal(right_high), block_diagonal(right_low)], axis=1)
    stacked = jnp.concatenate([query[:, lanes * j:lanes * (j + 1)] for j in range(pairs)], axis=0)
    both = matmul(stacked, factor)
    turned[...] = both[:, :lanes] + both[:, lanes:]

    pick = ones_where(iota((proj, proj), 1) == 2 * (iota((proj, proj), 0) % pairs) + iota((proj, proj), 0) // pairs)
    b, place = iota((proj, proj), 0), iota((proj, proj), 1)
    other, j = place // pairs, place % pairs
    even = ones_where(b == 2 * j + other)
    odd = ones_where(b == 2 * j + 1 - other)
    upper_rows = iota((proj, proj), 0) < pairs

    def arranged(part):
        picked = matmul(pick, part).astype(bf16)
        return jnp.where(upper_rows, matmul(picked, even), matmul(picked, odd)).astype(bf16)

    left_high, left_low = split(left[...])
    high, low = arranged(left_high), arranged(left_low)
    weights = jnp.concatenate([
        jnp.concatenate([high, high], axis=1),
        jnp.concatenate([low, jnp.zeros_like(low)], axis=1)], axis=0)
    group = 8
    first_half = iota((pairs, lanes * group), 1) % lanes < proj
    for start in range(0, rows, group):
        own = [turned[pl.ds(q, pairs, stride=rows), :] for q in range(start, start + group)]
        own_high, own_low = split(jnp.concatenate(own, axis=1))
        rolled_high, rolled_low = split(jnp.concatenate([pltpu.roll(v, proj, 1) for v in own], axis=1))
        value = matmul(weights, jnp.concatenate([own_high, rolled_high, own_low, rolled_low], axis=0))
        value = value[:proj] + value[proj:]
        value = jnp.where(first_half, value[:pairs], value[pairs:])
        for q in range(group):
            result[pl.ds((start + q) * pairs, pairs), :] = value[:, lanes * q:lanes * (q + 1)]
    for i in range(pairs):
        store(i, result[pl.ds(i, rows, stride=pairs), :].astype(bf16))


def kernel(query_ref, left_ref, right_ref, train_ref, out_ref, query, left_v, right_v, turned, result, held, heldx, train, trainx, acc, mine, stage_y, landed_y, stage_z, landed_z,
           stage_d, landed_d, in_sem, train_sem, trainx_sem, zs, zs2, zr, xs, xr, hs, hr, ps, pr,
           bs, bs2, br, axs, axr, ahs, ahr, aps, apr, ys, yr, ws, wr, ds, dr):
    g = lax.axis_index("layer")
    row = lax.axis_index("row")
    core = lax.rem(row, 2)
    z = lax.rem(row // 2, NZ)
    x = row // (2 * NZ)
    y = lax.rem(g, NY)
    zh = g // NY
    upper = z // 2
    zl = jnp.where(upper == 1, 3 - z, z)
    end = zl == 0
    inner = jnp.logical_not(end)
    right, left = lax.rem(x + 1, NX), lax.rem(x + NX - 1, NX)
    side = z + 1 - 2 * lax.rem(z, 2)
    across = 3 - z
    layers, rows, feat = query_ref.shape
    cols = held.shape[-1]
    few = rows // HALVES
    low, high = pl.ds(0, cols // 2), pl.ds(cols // 2, cols // 2)
    wide_low, wide_high = pl.ds(0, few), pl.ds(few, few)

    def device(xx, zz, cc):
        return (g, (xx * NZ + zz) * 2 + cc)

    def held_z(k):
        c = jnp.where(k == 0, zl, jnp.where(k == 1, 1 - zl, k))
        return jnp.where(upper == 1, 3 - c, c)

    def in_copies():
        return [pltpu.make_async_copy(src, dst, in_sem.at[n]) for n, (src, dst) in enumerate(
            ((query_ref, query), (left_ref, left_v), (right_ref, right_v)))]

    def train_copy(p):
        return pltpu.make_async_copy(
            train_ref.at[p, :, pl.ds(0, cols)], train.at[p], train_sem.at[p])

    def trainx_copy(q):
        return pltpu.make_async_copy(
            train_ref.at[q, :, pl.ds(feat - XCOLS, XCOLS)], trainx.at[q], trainx_sem.at[q])

    for copy in in_copies():
        copy.start()

    barrier = pltpu.get_barrier_semaphore()

    def greet(target):
        pl.semaphore_signal(barrier, inc=1, device_id=target, device_id_type=MESH)

    for other in (1 - zh, zh):
        for j in (2, 1, 3, 0):
            if other is not zh or j > 0:
                greet((other * NY + lax.rem(y + j, NY), row))
    greet(device(right, z, core))
    greet(device(left, z, core))
    greet(device(x, z, 1 - core))
    greet(device(x, side, core))
    greet(device(x, across, core))
    for p in range(layers):
        train_copy(p).start()
    for q in range(XPIECES):
        trainx_copy(q).start()

    for copy in in_copies():
        copy.wait()
    tiles = cols // 128
    for layer in range(layers):
        def store(i, value):
            if i < tiles:
                for h in range(HALVES):
                    held[z, h * layers + layer, core, x, :, 128 * i:128 * (i + 1)] = value[h * few:(h + 1) * few]
            else:
                at = 128 * (i - tiles)
                heldx[z, layer, core, x, :, at:at + 128] = value

        precondition(query.at[layer], left_v.at[layer], right_v.at[layer], turned, result, store)

    pl.semaphore_wait(barrier, 5 + NG - 1)

    def remote(ref, send_sem, recv_sem, target):
        return pltpu.make_async_remote_copy(
            src_ref=ref, dst_ref=ref, send_sem=send_sem, recv_sem=recv_sem,
            device_id=target, device_id_type=MESH)

    def xdev(d):
        return device(right if d == 0 else left, z, core)

    def xsrc(d):
        return left if d == 0 else right

    def part(d):
        return low if d == 0 else high

    def wide_part(d):
        return wide_low if d == 0 else wide_high

    partner = device(x, z, 1 - core)

    def to_side(k, k_there, p):
        return remote(held.at[held_z(k), p, core, x], zs.at[k_there, p], zr.at[k_there, p], device(x, side, core))

    def to_across(k, k_there, p):
        return remote(held.at[held_z(k), p, core, x], zs2.at[k_there, p], zr.at[k_there, p], device(x, across, core))

    def to_x(k, p, d):
        return remote(held.at[held_z(k), p, core, x], xs.at[d, k, p], xr.at[d, k, p], xdev(d))

    def from_x(k, p, d):
        return remote(held.at[held_z(k), p, core, xsrc(d)], xs.at[d, k, p], xr.at[d, k, p], xdev(d))

    def relay(k, p, d):
        return remote(held.at[held_z(k), p, core, xsrc(d), :, part(d)], hs.at[d, k, p], hr.at[d, k, p], xdev(d))

    def to_partner(k, p):
        return remote(held.at[held_z(k), p, core], ps.at[k, p], pr.at[k, p], partner)

    def wide_to_x(q, d):
        return remote(heldx.at[z, q, core, x], axs.at[d, q], axr.at[d, q], xdev(d))

    def wide_from_x(q, d):
        return remote(heldx.at[z, q, core, xsrc(d)], axs.at[d, q], axr.at[d, q], xdev(d))

    def wide_relay(q, d):
        return remote(heldx.at[z, q, core, xsrc(d), wide_part(d)], ahs.at[d, q], ahr.at[d, q], xdev(d))

    def wide_to_side(k, k_there, q):
        return remote(heldx.at[held_z(k), q, core], bs.at[k_there, q], br.at[k_there, q], device(x, side, core))

    def wide_to_across(k, k_there, q):
        return remote(heldx.at[held_z(k), q, core], bs2.at[k_there, q], br.at[k_there, q], device(x, across, core))

    def wide_to_partner(k, q):
        return remote(heldx.at[held_z(k), q, core], aps.at[k, q], apr.at[k, q], partner)

    def to_y(k, h, t, b, dy):
        return pltpu.make_async_remote_copy(
            src_ref=stage_y.at[k, h, t], dst_ref=landed_y.at[b, h, y], send_sem=ys.at[k, h, t],
            recv_sem=yr.at[b, h, y], device_id=(zh * NY + dy, row), device_id_type=MESH)

    def from_y(b, h, sy):
        return pltpu.make_async_remote_copy(
            src_ref=stage_y.at[0, 0, 0], dst_ref=landed_y.at[b, h, sy], send_sem=ys.at[0, 0, 0],
            recv_sem=yr.at[b, h, sy], device_id=(zh * NY + sy, row), device_id_type=MESH)

    def to_z(b, h):
        return pltpu.make_async_remote_copy(
            src_ref=stage_z.at[b, h], dst_ref=landed_z.at[b, h], send_sem=ws.at[b, h], recv_sem=wr.at[b, h],
            device_id=((1 - zh) * NY + y, row), device_id_type=MESH)

    def to_owner(h, xx, owner):
        return pltpu.make_async_remote_copy(
            src_ref=stage_d.at[h, xx], dst_ref=landed_d.at[h, g], send_sem=ds.at[h, xx], recv_sem=dr.at[h, g],
            device_id=(owner, row), device_id_type=MESH)

    def from_member(h, src):
        return pltpu.make_async_remote_copy(
            src_ref=stage_d.at[0, 0], dst_ref=landed_d.at[h, src], send_sem=ds.at[0, 0], recv_sem=dr.at[h, src],
            device_id=(src, row), device_id_type=MESH)

    for q in range(XPIECES):
        for d in range(2):
            wide_to_x(q, d).start()
    for p in range(PIECES):
        to_side(0, 1, p).start()

        @pl.when(inner)
        def _():
            to_across(0, 2, p).start()

    def along_z(i):
        early = i - 3
        late = i - 8

        @pl.when(jnp.logical_and(inner, jnp.logical_and(early >= 0, early < PIECES)))
        def _():
            to_side(1, 1, early).wait_recv()
            to_across(1, 3, early).start()
            to_across(2, 2, early).wait_recv()
            to_side(2, 2, early).start()

        @pl.when(jnp.logical_and(inner, jnp.logical_and(late >= 0, late < PIECES)))
        def _():
            to_across(3, 3, late).wait_recv()
            to_side(3, 3, late).start()

    def wide(i):
        @pl.when(i == 1)
        def _():
            for q in range(XPIECES):
                for d in range(2):
                    wide_from_x(q, d).wait_recv()
                    wide_relay(q, d).start()

        @pl.when(i == 3)
        def _():
            for q in range(XPIECES):
                for d in range(2):
                    wide_relay(q, d).wait_recv()
                wide_to_side(0, 1, q).start()

                @pl.when(inner)
                def _():
                    wide_to_across(0, 2, q).start()

                wide_to_partner(0, q).start()

        @pl.when(i == 7)
        def _():
            for q in range(XPIECES):
                @pl.when(inner)
                def _():
                    wide_to_across(2, 2, q).wait_recv()
                    wide_to_side(2, 2, q).start()
                    wide_to_partner(2, q).start()

        @pl.when(i == 8)
        def _():
            for q in range(XPIECES):
                wide_to_side(1, 1, q).wait_recv()

                @pl.when(inner)
                def _():
                    wide_to_across(1, 3, q).start()

                wide_to_partner(1, q).start()

        @pl.when(jnp.logical_and(i == 12, inner))
        def _():
            for q in range(XPIECES):
                wide_to_across(3, 3, q).wait_recv()
                wide_to_side(3, 3, q).start()
                wide_to_partner(3, q).start()

        @pl.when(jnp.logical_and(i == 13, end))
        def _():
            for q in range(XPIECES):
                wide_to_side(2, 2, q).wait_recv()
                wide_to_partner(2, q).start()

        @pl.when(jnp.logical_and(i == 17, end))
        def _():
            for q in range(XPIECES):
                wide_to_side(3, 3, q).wait_recv()
                wide_to_partner(3, q).start()

    def sums_of(xx):
        return [acc[pl.ds((c * NX + xx) * few, few), :] for c in range(2)]

    def send_sums(k, h):
        zz = held_z(k)
        b = lax.rem(zz, 2)

        @pl.when(k < NZ - 1)
        def _():
            for t in range(2):
                dy = 2 * t + zz // 2

                @pl.when(dy == y)
                def _():
                    for u in range(2):
                        for c, value in enumerate(sums_of(2 * u + t)):
                            mine[b, h, u, pl.ds(c * few, few), :] = value

                @pl.when(dy != y)
                def _():
                    for u in range(2):
                        for c, value in enumerate(sums_of(2 * u + t)):
                            stage_y[k, h, t, u, pl.ds(c * few, few), :] = value.astype(jnp.bfloat16)
                    to_y(k, h, t, b, dy).start()

        @pl.when(k == NZ - 1)
        def _():
            for n in range(NX):
                xx = lax.rem(n + 2 * (1 - zh), NX)
                owner = 2 * xx + zz // 2
                pieces = [acc[pl.ds(pl.multiple_of((c * NX + xx) * few, few), few), :] for c in range(2)]

                @pl.when(owner == g)
                def _():
                    for c, value in enumerate(pieces):
                        mine[b, h, zh, pl.ds(c * few, few), :] = value

                @pl.when(owner != g)
                def _():
                    for c, value in enumerate(pieces):
                        stage_d[h, xx, pl.ds(c * few, few), :] = value.astype(jnp.bfloat16)
                    to_owner(h, xx, owner).start()

    def reduce_y(i):
        n = i - AT_SUM
        k, h = n // PIECES, lax.rem(n + PIECES, PIECES) // layers

        @pl.when(jnp.logical_and(n >= 0, jnp.logical_and(lax.rem(n + PIECES, layers) == 0, k < NZ - 1)))
        def _():
            zz = held_z(k)
            b = lax.rem(zz, 2)

            @pl.when(zz // 2 == lax.rem(y, 2))
            def _():
                for j in range(1, NY):
                    from_y(b, h, lax.rem(y + j, NY)).wait_recv()

                def total(u):
                    value = mine[b, h, u]
                    for j in range(1, NY):
                        value = value + landed_y[b, h, lax.rem(y + j, NY), u].astype(jnp.float32)
                    return value

                stage_z[b, h] = total(1 - zh).astype(jnp.bfloat16)
                to_z(b, h).start()
                mine[b, h, zh] = total(zh)

    def step(i, carry):
        along_z(i)
        wide(i)

        @pl.when(i < STEPS)
        def _():
            k, p = i // PIECES, lax.rem(i, PIECES)

            @pl.when(jnp.logical_and(end, k > 0))
            def _():
                to_side(k, k, p).wait_recv()

            to_x(k, p, 0).start()
            to_x(k, p, 1).start()

        @pl.when(jnp.logical_and(i >= AT_B, i < STEPS + AT_B))
        def _():
            s = i - AT_B
            k, p = s // PIECES, lax.rem(s, PIECES)
            from_x(k, p, 0).wait_recv()
            relay(k, p, 0).start()
            from_x(k, p, 1).wait_recv()
            relay(k, p, 1).start()

        @pl.when(jnp.logical_and(i >= AT_C, i < STEPS + AT_C))
        def _():
            s = i - AT_C
            k, p = s // PIECES, lax.rem(s, PIECES)
            relay(k, p, 0).wait_recv()
            relay(k, p, 1).wait_recv()
            to_partner(k, p).start()

        @pl.when(i >= AT_D)
        def _():
            s = i - AT_D
            k, p = s // PIECES, lax.rem(s, PIECES)

            h, layer = p // layers, lax.rem(p, layers)

            def product(lhs, rhs):
                return lax.dot_general(lhs.reshape(2 * NX * few, lhs.shape[-1]), rhs, (((1,), (1,)), ((), ())),
                                       preferred_element_type=jnp.float32)

            @pl.when(s == 0)
            def _():
                for q in range(XPIECES):
                    trainx_copy(q).wait()

            @pl.when(s < layers)
            def _():
                pltpu.make_async_copy(train.at[layer], train.at[layer], train_sem.at[layer]).wait()

            to_partner(k, p).wait_recv()
            term = product(held[held_z(k), p], train[layer])

            @pl.when(layer == 0)
            def _():
                acc[...] = term

            @pl.when(layer > 0)
            def _():
                acc[...] += term

            @pl.when(jnp.logical_or(p == layers - 1, p == layers))
            def _():
                for q in range(XPIECES):
                    @pl.when(h == 0)
                    def _():
                        wide_to_partner(k, q).wait_recv()

                    acc[...] += product(heldx[held_z(k), q, :, :, pl.ds(pl.multiple_of(h * few, few), few), :], trainx[q])

            @pl.when(layer == layers - 1)
            def _():
                send_sums(k, h)

        reduce_y(i)
        return carry

    lax.fori_loop(0, STEPS + AT_D, step, 0)

    def drain(s, carry):
        k, p = s // PIECES, lax.rem(s, PIECES)
        for d in range(2):
            to_x(k, p, d).wait_send()
            relay(k, p, d).wait_send()
        to_partner(k, p).wait_send()

        @pl.when(k == 0)
        def _():
            to_side(0, 1, p).wait_send()

        @pl.when(inner)
        def _():
            @pl.when(k == 0)
            def _():
                to_across(0, 2, p).wait_send()

            @pl.when(k == 1)
            def _():
                to_across(1, 3, p).wait_send()

            @pl.when(k >= 2)
            def _():
                to_side(k, k, p).wait_send()

        return carry

    lax.fori_loop(0, STEPS, drain, 0)
    for q in range(XPIECES):
        for d in range(2):
            wide_to_x(q, d).wait_send()
            wide_relay(q, d).wait_send()
        wide_to_side(0, 1, q).wait_send()
        for k in range(NZ):
            wide_to_partner(k, q).wait_send()

        @pl.when(inner)
        def _():
            wide_to_across(0, 2, q).wait_send()
            wide_to_across(1, 3, q).wait_send()
            wide_to_side(2, 2, q).wait_send()
            wide_to_side(3, 3, q).wait_send()

    for h in range(HALVES):
        for k in range(NZ - 1):
            zz = held_z(k)
            for t in range(2):
                @pl.when(2 * t + zz // 2 != y)
                def _():
                    to_y(k, h, t, 0, 0).wait_send()

    late_owner = lax.rem(y, 2) != upper
    last_b = lax.rem(held_z(NZ - 1), 2)
    for h in range(HALVES):
        for b in range(2):
            direct = jnp.logical_and(late_owner, last_b == b)

            def put(value):
                for c in range(2):
                    out_ref[pl.ds(b * 2 * rows + c * rows + h * few, few), :] = value[c * few:(c + 1) * few]

            @pl.when(jnp.logical_not(direct))
            def _():
                to_z(b, h).wait_recv()
                put(mine[b, h, zh] + landed_z[b, h].astype(jnp.float32))

            @pl.when(direct)
            def _():
                value = mine[b, h, zh]
                for j in range(1, NG):
                    src = lax.rem(g + j, NG)
                    from_member(h, src).wait_recv()
                    value = value + landed_d[h, src].astype(jnp.float32)
                put(value)

    for h in range(HALVES):
        for b in range(2):
            @pl.when(jnp.logical_not(jnp.logical_and(late_owner, last_b == b)))
            def _():
                to_z(b, h).wait_send()

        for xx in range(NX):
            @pl.when(2 * xx + held_z(NZ - 1) // 2 != g)
            def _():
                to_owner(h, xx, 0).wait_send()


def on_device(query_grads, train_grads, left_inverse, right_inverse):
    layers, rows, feat = query_grads.shape
    proj = left_inverse.shape[1]
    train_rows = train_grads.shape[1]
    cols = feat - XCOLS
    few = rows // HALVES
    block = NX * NZ * 2 * rows // NG
    dma = pltpu.SemaphoreType.DMA
    bf16, f32 = jnp.bfloat16, jnp.float32
    return pl.pallas_call(
        kernel,
        out_shape=pltpu.VMEM((block, train_rows), f32),
        in_specs=[pl.BlockSpec(memory_space=pl.ANY)] * 4,
        out_specs=pl.BlockSpec(memory_space=pltpu.VMEM),
        scratch_shapes=[
            pltpu.VMEM((layers, rows, feat), bf16),
            pltpu.VMEM((layers, proj, proj), f32),
            pltpu.VMEM((layers, proj, proj), f32),
            pltpu.VMEM((rows * proj // 2, 2 * proj), f32),
            pltpu.VMEM((rows * proj // 2, 2 * proj), f32),
            pltpu.VMEM((NZ, PIECES, 2, NX, few, cols), bf16),
            pltpu.VMEM((NZ, XPIECES, 2, NX, rows, XCOLS), bf16),
            pltpu.VMEM((layers, train_rows, cols), bf16),
            pltpu.VMEM((XPIECES, train_rows, XCOLS), bf16),
            pltpu.VMEM((2 * NX * few, train_rows), f32),
            pltpu.VMEM((2, HALVES, 2, 2 * few, train_rows), f32),
            pltpu.VMEM((NZ - 1, HALVES, 2, 2, 2 * few, train_rows), bf16),
            pltpu.VMEM((2, HALVES, NY, 2, 2 * few, train_rows), bf16),
            pltpu.VMEM((2, HALVES, 2 * few, train_rows), bf16),
            pltpu.VMEM((2, HALVES, 2 * few, train_rows), bf16),
            pltpu.VMEM((HALVES, NX, 2 * few, train_rows), bf16),
            pltpu.VMEM((HALVES, NG, 2 * few, train_rows), bf16),
            dma((3,)), dma((layers,)), dma((XPIECES,)),
            dma((NZ, PIECES)), dma((NZ, PIECES)), dma((NZ, PIECES)),
            dma((2, NZ, PIECES)), dma((2, NZ, PIECES)), dma((2, NZ, PIECES)), dma((2, NZ, PIECES)),
            dma((NZ, PIECES)), dma((NZ, PIECES)),
            dma((NZ, XPIECES)), dma((NZ, XPIECES)), dma((NZ, XPIECES)),
            dma((2, XPIECES)), dma((2, XPIECES)), dma((2, XPIECES)), dma((2, XPIECES)),
            dma((NZ, XPIECES)), dma((NZ, XPIECES)),
            dma((NZ - 1, HALVES, 2)), dma((2, HALVES, NY)), dma((2, HALVES)), dma((2, HALVES)),
            dma((HALVES, NX)), dma((HALVES, NG)),
        ],
        compiler_params=pltpu.CompilerParams(
            collective_id=0, has_side_effects=True, vmem_limit_bytes=60 * 1024 * 1024),
    )(query_grads, left_inverse, right_inverse, train_grads)


def solution(mesh):
    placed = (
        P("layer", "row", None),
        P("layer", "row", None),
        P("layer", None, None),
        P("layer", None, None),
    )
    return jax.shard_map(
        on_device, mesh=mesh, in_specs=placed, out_specs=P("layer", "row"), check_vma=False
    )
```
